32 devices in a mesh: grp: 2 (over y), col: 8 (over z, x), row: 2 (over core).
Axes of the slice: x: 2, y: 2, z: 4, core: 2. Of those that a mesh axis runs over, the one named last changes fastest.
Arguments:
- pair_block: float32 [4, 16, 1152, 128], P('grp', 'row', 'col'), parts along dimension 0, may hold values from -260 to 260
- query_single: bfloat16 [4, 16, 768], P('grp', 'row'), parts along dimension 0, may hold values from -70 to 70
- key_single: bfloat16 [2304, 768], P(('grp', 'col')), parts along dimension 0, may hold values from -70 to 70
- query_chain: int32 [4, 16], P('grp', 'row'), parts along dimension 0, may hold values from 0 to 23
- key_chain: int32 [2304], P(('grp', 'col')), parts along dimension 0, may hold values from 0 to 23, never falling along the last dimension, each value on 1 to 144 neighbouring positions
- query_mask: int32 [4, 16], P('grp', 'row'), parts along dimension 0, may hold values 0 or 1
- key_mask: int32 [2304], P(('grp', 'col')), parts along dimension 0, may hold values 0 or 1
- timestep: int32 [2], P('grp'), parts along dimension 0, may hold values from 0 to 49
- time_table: bfloat16 [50, 768], replicated, may hold values from -6 to 6
- norm_gain: float32 [768], replicated, may hold values from 0.1 to 1.9
- left_proj: bfloat16 [768, 8], replicated, may hold values from -0.21875 to 0.21875
- right_proj: bfloat16 [768, 8], replicated, may hold values from -0.21875 to 0.21875
- outer_proj: bfloat16 [64, 128], replicated, may hold values from -0.75 to 0.75
- bias_proj: float32 [128, 12], replicated, may hold values from -0.75 to 0.75
- chain_weight: float32 [12], replicated, may hold values from -2 to 2
- query_proj: bfloat16 [768, 1536], P(None, 'col'), may hold values from -0.21875 to 0.21875
- kv_proj: bfloat16 [768, 1536], P(None, 'row'), may hold values from -0.21875 to 0.21875
- out_proj: bfloat16 [768, 768], replicated, may hold values from -0.75 to 0.75
Outputs:
- new_pair: float32 [4, 16, 1152, 128], P('grp', 'row', 'col'), parts along dimension 0
- single_update: bfloat16 [4, 16, 768], P('grp', 'row'), parts along dimension 0
The draws below stay inside these ranges and needn't reach their ends.
There are 2 independent parts, one for each index of `grp`. The reference program is written for one: setup_inputs(seed, part) draws one part's arguments, and reference() takes and returns one part's arrays. A program takes and returns all parts, laid end to end along the dimension named above; an argument that names none is the same for every part. Nothing has to cross between parts.
Inputs may be any that keep to these rules, and one draw needn't show every extreme that they name: `key_chain`: never falling along the residues; each of the 24 chains holds at least one residue.
All inputs are finite; a program needn't handle non-finite values. No bound on the sum of `query_mask` or of `key_mask` on one device may be relied on, other than what follows from the above.
Results may differ from the reference program's by a relative error of at most 0.0082.
Values may be sent and summed in bfloat16 or wider, within the bound.
No kernel may reach another device: no remote copies, remote signals or barrier semaphores. Data moves between devices by JAX's collectives and lax.ppermute only.
A program may use at most 64 MiB of HBM per device.

```python
import math
import jax
import jax.numpy as jnp
import numpy as np
from jax import lax

HEADS = 12
HEAD_DIM = 64
C = 128
RANK = 8
STEPS = 50
CHAINS = 24
SLABS = 2
D = 768
SLAB_ROWS = 16
RES = 1152


def scaled_entries(key, full_shape):
    return jnp.clip(jax.random.normal(key, full_shape, jnp.float32), -6.0, 6.0)


def draw_query_single(key, part):
    return scaled_entries(jax.random.fold_in(key, 11), (SLABS, SLAB_ROWS, D)).astype(jnp.bfloat16)


def draw_key_single(key, part):
    return scaled_entries(jax.random.fold_in(key, 12), (RES, D)).astype(jnp.bfloat16)


def draw_pair_block(key, part):
    base_key = jax.random.fold_in(key, 13)
    full_shape = (SLABS, SLAB_ROWS, RES, C)
    return jnp.clip(jax.random.normal(base_key, full_shape, jnp.float32), -6.0, 6.0)


def with_ends(array, own_key, least, top_value):
    extent = array.shape
    place = [jax.random.randint(jax.random.fold_in(own_key, axis), (), 0, extent[axis]) for axis in range(len(extent))]
    array = array.at[tuple(place)].set(least)
    longest = extent.index(max(extent))
    place[longest] = (place[longest] + 1) % extent[longest]
    return array.at[tuple(place)].set(top_value)


def steps_of(key, shape, cuts, low, largest):
    level = 1.0
    for axis_at, shards_of in cuts:
        steps = jax.random.uniform(jax.random.fold_in(jax.random.fold_in(key, 6), axis_at), (shards_of,), jnp.float32, low / len(cuts), largest / len(cuts))
        level = level * jnp.repeat(jnp.exp(steps), shape[axis_at] // shards_of).reshape((-1,) + (1,) * (len(shape) - 1 - axis_at))
    return level


def length_profile(number_of, total, bound, lean):
    loads = [(1 << 20) // math.isqrt(standing ** lean) + 1 for standing in range(2, number_of + 1)]
    rest, counts = total - bound - (number_of - 1), [1] * (number_of - 1)
    while rest > 0:
        candidates = [i for i in range(number_of - 1) if counts[i] < bound]
        pool, left = sum([loads[i] for i in candidates]), rest
        for i in candidates:
            more = min(bound - counts[i], max(1, left * loads[i] // pool), rest)
            counts[i] = counts[i] + more
            rest = rest - more
    return np.array([bound] + counts)


def ragged(stream_key, count, total, bound, slope):
    if count == 2:
        one = jax.random.randint(stream_key, (), max(1, total - bound), min(bound, total - 1) + 1)
        return jnp.stack([one, total - one])
    tallies = jnp.asarray(length_profile(count, total, bound, slope), jnp.int32)
    twos = (count - 1) // 2
    giver, receiver = tallies[1:1 + 2 * twos:2], tallies[2:2 + 2 * twos:2]
    slack = jnp.minimum(giver - 1, bound - receiver)
    shifted = jax.random.randint(jax.random.fold_in(stream_key, 1), (twos,), 0, 1 << 20) % (slack + 1)
    tallies = tallies.at[1:1 + 2 * twos:2].set(giver - shifted).at[2:2 + 2 * twos:2].set(receiver + shifted)
    return tallies[jax.random.permutation(jax.random.fold_in(stream_key, 2), count)]


def bell_draw(key, dims, scale, most, pieces=(), kind=jnp.bfloat16):
    drawn = scale * jax.random.normal(key, dims, jnp.float32)
    if pieces:
        drawn = drawn * steps_of(key, dims, pieces, -0.22, 0.18)
    return jnp.clip(drawn, -most, most).astype(kind)


def setup_inputs(seed: int = 0, part: int = 0) -> dict:
    streams_of = jax.random.split(jax.random.key(seed), 19)
    part_keys = jax.random.split(jax.random.fold_in(streams_of[18], part), 19)
    pair_block = draw_pair_block(jax.random.fold_in(jax.random.fold_in(streams_of[18], part), 71), part)
    query_single = draw_query_single(jax.random.fold_in(jax.random.fold_in(streams_of[18], part), 71), part)
    key_single = draw_key_single(jax.random.fold_in(jax.random.fold_in(streams_of[18], part), 71), part)
    query_chain = with_ends(jax.random.randint(part_keys[3], (SLABS, SLAB_ROWS), 0, CHAINS), jax.random.fold_in(part_keys[3], 1), 0, CHAINS - 1).astype(jnp.int32)
    key_chain = jnp.searchsorted(jnp.cumsum(ragged(part_keys[4], CHAINS, RES, RES // 8, 0)), jnp.arange(RES), side="right").astype(jnp.int32)
    query_mask = with_ends((jax.random.randint(part_keys[5], (SLABS, SLAB_ROWS), 0, 2) < 1).astype(jnp.int32), jax.random.fold_in(part_keys[5], 1), 0, 1)
    key_mask = with_ends((jax.random.randint(part_keys[6], (RES,), 0, 2) < 1).astype(jnp.int32), jax.random.fold_in(part_keys[6], 1), 0, 1)
    timestep = jax.random.randint(part_keys[7], (1,), 0, STEPS).astype(jnp.int32)
    time_table = bell_draw(streams_of[8], (STEPS, D), 1.0, 6.0)
    norm_gain = jnp.clip(1.0 + 0.18 * jax.random.normal(streams_of[9], (D,), jnp.float32), 0.1, 1.9)
    left_proj = bell_draw(streams_of[10], (D, RANK), D ** -0.5, 0.21875)
    right_proj = bell_draw(streams_of[11], (D, RANK), D ** -0.5, 0.21875)
    outer_proj = bell_draw(streams_of[12], (RANK * RANK, C), (RANK * RANK) ** -0.5, 0.75)
    bias_proj = bell_draw(streams_of[13], (C, HEADS), (C // 2) ** -0.5, 0.75, (), jnp.float32)
    chain_weight = jnp.clip(jax.random.uniform(streams_of[14], (HEADS,), jnp.float32, -2.0, 2.0), -2.0, 2.0)
    query_proj = bell_draw(streams_of[15], (D, 2 * D), D ** -0.5, 0.21875, ((1, 8),))
    kv_proj = bell_draw(streams_of[16], (D, 2 * D), D ** -0.5, 0.21875, ((1, 2),))
    out_proj = bell_draw(streams_of[17], (D, D), HEAD_DIM ** -0.5, 0.75)
    return dict(pair_block=pair_block, query_single=query_single, key_single=key_single, query_chain=query_chain, key_chain=key_chain, query_mask=query_mask, key_mask=key_mask, timestep=timestep, time_table=time_table, norm_gain=norm_gain, left_proj=left_proj, right_proj=right_proj, outer_proj=outer_proj, bias_proj=bias_proj, chain_weight=chain_weight, query_proj=query_proj, kv_proj=kv_proj, out_proj=out_proj)


EPSILON = 1e-05
HIGHEST = lax.Precision.HIGHEST

def normalize(features, norm_gain):
    average = lax.optimization_barrier(jnp.mean(features, axis=-1, keepdims=True))
    centred = features - average
    spread = lax.optimization_barrier(jnp.mean(centred * centred, axis=-1, keepdims=True))
    return (centred * lax.rsqrt(spread + EPSILON) * norm_gain).astype(jnp.bfloat16)

def wide_dot(left, right):
    return jnp.dot(left.astype(jnp.float32), right.astype(jnp.float32), precision=HIGHEST, preferred_element_type=jnp.float32)

def flat_dot(left, right):
    flat_left = left.reshape(-1, left.shape[-1])
    product = wide_dot(flat_left, right)
    return product.reshape(left.shape[:-1] + (right.shape[-1],))

def reference(pair_block, query_single, key_single, query_chain, key_chain, query_mask, key_mask, timestep, time_table, norm_gain, left_proj, right_proj, outer_proj, bias_proj, chain_weight, query_proj, kv_proj, out_proj):
    picked = jnp.arange(STEPS, dtype=jnp.int32) == timestep[0]
    time_row = lax.optimization_barrier(jnp.sum(jnp.where(picked[:, None], time_table.astype(jnp.float32), jnp.float32(0.0)), axis=0))
    query_norm = normalize(query_single.astype(jnp.float32) + query_mask[:, :, None].astype(jnp.float32) * time_row, norm_gain)
    key_norm = normalize(key_single.astype(jnp.float32) + key_mask[:, None].astype(jnp.float32) * time_row, norm_gain)
    query_gate = lax.optimization_barrier(flat_dot(query_norm, query_proj).astype(jnp.bfloat16))
    keys_values = lax.optimization_barrier(wide_dot(key_norm, kv_proj).astype(jnp.bfloat16))
    left_factor = flat_dot(query_norm, left_proj)
    right_factor = wide_dot(key_norm, right_proj)
    mixer = jnp.einsum('sra,abc->srbc', left_factor, outer_proj.astype(jnp.float32).reshape(RANK, RANK, C), precision=HIGHEST)
    new_pair = pair_block + jnp.einsum('jb,srbc->srjc', right_factor, mixer, precision=HIGHEST)
    differ = (query_chain[:, :, None] != key_chain[None, None, :]).astype(jnp.float32)
    logit_bias = jnp.einsum('srjc,ch->srhj', new_pair, bias_proj, precision=HIGHEST) + chain_weight[None, None, :, None] * differ[:, :, None, :]
    query_heads = query_gate[:, :, :D].astype(jnp.float32).reshape(SLABS, SLAB_ROWS, HEADS, HEAD_DIM)
    key_heads = keys_values[:, :D].astype(jnp.float32).reshape(RES, HEADS, HEAD_DIM)
    value_heads = keys_values[:, D:].astype(jnp.float32).reshape(RES, HEADS, HEAD_DIM)
    scores = jnp.einsum('srhd,jhd->srhj', query_heads, key_heads, precision=HIGHEST) * (1.0 / math.sqrt(HEAD_DIM)) + logit_bias
    maxima = lax.optimization_barrier(jnp.max(scores, axis=-1, keepdims=True))
    exponent = jnp.exp(scores - maxima)
    totals = lax.optimization_barrier(jnp.sum(exponent, axis=-1))
    weights = lax.optimization_barrier(exponent.astype(jnp.bfloat16)).astype(jnp.float32)
    summed = jnp.einsum('srhj,jhd->srhd', weights, value_heads, precision=HIGHEST)
    gate_factor = jax.nn.sigmoid(query_gate[:, :, D:].astype(jnp.float32))
    attended = ((summed / totals[..., None]).reshape(SLABS, SLAB_ROWS, D) * gate_factor).astype(jnp.bfloat16)
    single_update = flat_dot(attended, out_proj).astype(jnp.bfloat16)
    return (new_pair, single_update)
```

```python
import functools
import math

import jax
import jax.numpy as jnp
from jax import lax
from jax.experimental import pallas as pl
from jax.experimental.pallas import tpu as pltpu
from jax.sharding import PartitionSpec as P

EPSILON = 1e-05
HIGHEST = lax.Precision.HIGHEST
LANES = 128
VMEM = pl.BlockSpec(memory_space=pltpu.VMEM)
SMEM = pl.BlockSpec(memory_space=pltpu.SMEM)
F32 = jnp.float32
BF16 = jnp.bfloat16


def dot(left, right, precision=None):
    return jnp.dot(left, right, preferred_element_type=F32, precision=precision)


def dot_nt(left, right):
    return lax.dot_general(left, right, (((1,), (1,)), ((), ())), preferred_element_type=F32)


def dot_tn(left, right):
    return lax.dot_general(left, right, (((0,), (0,)), ((), ())), preferred_element_type=F32)


def iota(shape, axis):
    return lax.broadcasted_iota(jnp.int32, shape, axis)


def split(value):
    high = value.astype(BF16)
    return high, (value - high.astype(F32)).astype(BF16)


def pick_time(step_ref, table_ref):
    table = table_ref[...].astype(F32)
    return jnp.sum(jnp.where(iota(table.shape, 0) == step_ref[0], table, 0.0), axis=0, keepdims=True)


def normalized(features, gain):
    average = jnp.mean(features, axis=-1, keepdims=True)
    centred = features - average
    spread = jnp.mean(centred * centred, axis=-1, keepdims=True)
    return (centred * lax.rsqrt(spread + EPSILON) * gain).astype(BF16)


def column_of(row):
    count = row.shape[1]
    square = (count, count)
    return jnp.sum(jnp.where(iota(square, 0) == iota(square, 1), row, 0), axis=1, keepdims=True)


def query_kernel(step, mask, single, table, gain, proj, part_out, norm_out):
    slabs, rows, width = single.shape
    count = slabs * rows
    features = single[...].astype(F32).reshape(count, width)
    place = iota((count, 1), 0)
    kept = jnp.zeros((count, 1), F32)
    for index in range(count):
        kept = jnp.where(place == index, mask[index // rows, index % rows].astype(F32), kept)
    norm = normalized(features + kept * pick_time(step, table), gain[...])
    norm_out[...] = norm
    part_out[...] = dot(norm, proj[...]).astype(BF16)


def key_kernel(step, mask, single, table, gain, proj, right_proj, half_out, right_out):
    kept = column_of(mask[...].astype(F32))
    features = single[...].astype(F32) + kept * pick_time(step, table)
    norm = normalized(features, gain[...])
    half_out[...] = dot(norm, proj[...]).astype(BF16)
    right_out[...] = dot(norm, right_proj[...])


def pair_kernel(
    chain_weight,
    query_chain,
    query_norm,
    left_proj,
    outer_proj,
    bias_proj,
    right,
    key_chain,
    pair,
    pair_out,
    bias_out,
    mixer_scratch,
    spread_scratch,
    weight_scratch,
):
    step = pl.program_id(0)
    count = query_norm.shape[0]
    rank = left_proj.shape[1]
    channels, heads = bias_proj.shape
    key_count = right.shape[0]
    lanes = heads * count
    block = pair.shape[1]

    @pl.when(step == 0)
    def _():
        left = dot(query_norm[...], left_proj[...])
        repeated = (iota((rank, rank * rank), 1) // rank == iota((rank, rank * rank), 0)).astype(F32)
        wide = dot(left, repeated, HIGHEST)
        tall = jnp.broadcast_to(wide[:, None, :], (count, rank, rank * rank))
        tall = tall.reshape(count * rank, rank * rank)
        spot = (count * rank, rank * rank)
        tall = jnp.where(iota(spot, 0) % rank == iota(spot, 1) % rank, tall, 0.0)
        mixer = dot(tall, outer_proj[...].astype(F32), HIGHEST).reshape(count, rank, channels)
        high, low = split(mixer)
        mixer_scratch[:, :rank, :] = high.astype(F32)
        mixer_scratch[:, rank : 2 * rank, :] = high.astype(F32)
        mixer_scratch[:, 2 * rank :, :] = low.astype(F32)
        high, low = split(right[...])
        spread_scratch[...] = jnp.concatenate(
            [high.astype(F32), low.astype(F32), high.astype(F32)], axis=1
        )
        expand = (iota((heads, lanes), 1) // count == iota((heads, lanes), 0)).astype(F32)
        high, low = split(dot(bias_proj[...], expand, HIGHEST))
        weight_scratch[0] = high
        weight_scratch[1] = low
        lane = iota((1, lanes), 1)
        weights = jnp.zeros((1, lanes), F32)
        for head in range(heads):
            weights = jnp.where(lane // count == head, chain_weight[head], weights)
        chains = jnp.zeros((1, lanes), jnp.int32)
        rows = query_chain.shape[1]
        for index in range(count):
            chains = jnp.where(lane % count == index, query_chain[index // rows, index % rows], chains)
        own = column_of(key_chain[...])
        bias_out[...] = jnp.where(own != chains, weights, 0.0)

    lane = iota((key_count, lanes), 1)
    spread = spread_scratch[...].astype(BF16)
    total = bias_out[...]
    for index in range(block):
        mixer = mixer_scratch[step * block + index].astype(BF16)
        fresh = pair[0, index] + dot(spread, mixer)
        pair_out[0, index] = fresh
        high, low = split(fresh)
        here = dot(high, weight_scratch[0]) + dot(high, weight_scratch[1]) + dot(low, weight_scratch[0])
        total = jnp.where(lane % count == step * block + index, total + here, total)
    bias_out[...] = total


def attend_kernel(place, pieces, own, other, bias, part_out, heads, count, mask_count):
    col, row = place[0], place[1]
    model = own.shape[1]
    head = model // heads
    share = pieces[0].shape[1]
    if len(pieces) > 1:
        blocks = []
        for target in range(model // share):
            chosen = pieces[0][...]
            for index in range(1, len(pieces)):
                chosen = jnp.where((col ^ target) == index, pieces[index][...], chosen)
            blocks.append(chosen)
        query = jnp.concatenate(blocks, axis=1)
    else:
        query = pieces[0][:, :model]
    first, second = own[...], other[...]
    keys = jnp.where(row == 0, first, second)
    values = jnp.where(row == 0, second, first)
    lane = iota((count, model), 1)
    spread = jnp.concatenate(
        [jnp.where(lane // head == index, query, jnp.zeros_like(query)) for index in range(heads)],
        axis=0,
    )
    scores = dot_nt(keys, spread) * (1.0 / math.sqrt(head)) + bias[...]
    peak = jnp.max(scores, axis=0, keepdims=True)
    exponent = jnp.exp(scores - peak)
    total = jnp.sum(exponent, axis=0, keepdims=True)
    summed = dot_tn(exponent.astype(BF16), values)
    lanes = heads * count
    spot = (count, lanes)
    keep = iota(spot, 1) % count == iota(spot, 0)
    gather = (iota((lanes, LANES), 0) // count == iota((lanes, LANES), 1)).astype(F32)
    stats = jnp.concatenate([jnp.where(keep, peak, 0.0), jnp.where(keep, total, 0.0)], axis=0)
    stats = dot(stats, gather, HIGHEST)
    taken = jnp.zeros((count, model), F32)
    for index in range(heads):
        taken = jnp.where(lane // head == index, summed[index * count : (index + 1) * count], taken)
    part_out[:, :model] = taken
    part_out[:, model : model + LANES] = stats[:count]
    part_out[:, model + LANES :] = stats[count:]


def merged(parts, heads):
    model = parts[0].shape[1] - 2 * LANES
    count = parts[0].shape[0]
    peak = functools.reduce(jnp.maximum, [part[:, model : model + LANES] for part in parts])
    scales = [jnp.exp(part[:, model : model + LANES] - peak) for part in parts]
    total = sum(scale * part[:, model + LANES :] for scale, part in zip(scales, parts))
    widen = (iota((LANES, model), 1) // (model // heads) == iota((LANES, model), 0)).astype(F32)
    wide = dot(jnp.concatenate(scales + [total], axis=0), widen, HIGHEST)
    summed = sum(
        wide[index * count : (index + 1) * count] * part[:, :model] for index, part in enumerate(parts)
    )
    return summed, peak, total, wide[len(parts) * count :]


def join_kernel(first, second, part_out, heads):
    summed, peak, total, _ = merged([first[...], second[...]], heads)
    model = summed.shape[1]
    part_out[:, :model] = summed
    part_out[:, model : model + LANES] = peak
    part_out[:, model + LANES :] = total


def finish_kernel(place, pieces, parts, out_proj, update_out, heads):
    col = place[0]
    model = out_proj.shape[0]
    share = pieces[0].shape[1]
    if len(pieces) > 1:
        blocks = []
        for target in range(model // share, 2 * model // share):
            chosen = pieces[0][...]
            for index in range(1, len(pieces)):
                chosen = jnp.where((col ^ target) == index, pieces[index][...], chosen)
            blocks.append(chosen)
        gate = jnp.concatenate(blocks, axis=1)
    else:
        gate = pieces[0][:, model:]
    values = []
    for part in parts:
        values += [part[...]] if len(part.shape) == 2 else [part[i] for i in range(part.shape[0])]
    summed, _, _, total = merged(values, heads)
    attended = (summed / total * jax.nn.sigmoid(gate.astype(F32))).astype(BF16)
    update_out[...] = dot(attended, out_proj[...]).astype(BF16)


def exchanged(value, axis, flip):
    size = lax.axis_size(axis)
    return lax.ppermute(value, axis, [(index, index ^ flip) for index in range(size)])


def on_device(
    pair_block,
    query_single,
    key_single,
    query_chain,
    key_chain,
    query_mask,
    key_mask,
    timestep,
    time_table,
    norm_gain,
    left_proj,
    right_proj,
    outer_proj,
    bias_proj,
    chain_weight,
    query_proj,
    kv_proj,
    out_proj,
):
    slabs, rows, model = query_single.shape
    count = slabs * rows
    key_count = key_single.shape[0]
    heads = chain_weight.shape[0]
    channels = pair_block.shape[-1]
    rank = left_proj.shape[1]
    lanes = heads * count
    cols = lax.axis_size("col")
    gain = norm_gain.reshape(1, model)
    place = jnp.stack([lax.axis_index("col"), lax.axis_index("row")]).astype(jnp.int32)

    query_part, query_norm = pl.pallas_call(
        query_kernel,
        out_shape=(
            jax.ShapeDtypeStruct((count, query_proj.shape[1]), BF16),
            jax.ShapeDtypeStruct((count, model), BF16),
        ),
        in_specs=[SMEM, SMEM] + [VMEM] * 4,
        out_specs=(VMEM, VMEM),
        name="query",
    )(timestep, query_mask, query_single, time_table, gain, query_proj)

    half, right = pl.pallas_call(
        key_kernel,
        out_shape=(
            jax.ShapeDtypeStruct((key_count, kv_proj.shape[1]), BF16),
            jax.ShapeDtypeStruct((key_count, rank), F32),
        ),
        in_specs=[SMEM] + [VMEM] * 6,
        out_specs=(VMEM, VMEM),
        name="keys",
    )(
        timestep,
        key_mask.reshape(1, key_count),
        key_single,
        time_table,
        gain,
        kv_proj,
        right_proj,
    )
    other = exchanged(half, "row", 1)

    direct = cols == 8
    if direct:
        near = exchanged(query_part, "col", 1)
        both = jnp.stack([query_part, near])
        pieces = [query_part, near]
        for flip in (2, 4, 6):
            far = exchanged(both, "col", flip)
            pieces += [far[0], far[1]]
    else:
        pieces = [lax.all_gather(query_part, "col", axis=1, tiled=True)]

    steps = 4
    block = count // steps
    per_slab = rows // block
    whole = lambda *shape: pl.BlockSpec(shape, lambda i: (0,) * len(shape))
    pair_spec = pl.BlockSpec(
        (1, block, key_count, channels), lambda i: (i // per_slab, i % per_slab, 0, 0)
    )
    new_pair, bias = pl.pallas_call(
        pair_kernel,
        grid=(steps,),
        out_shape=(
            jax.ShapeDtypeStruct(pair_block.shape, F32),
            jax.ShapeDtypeStruct((key_count, lanes), F32),
        ),
        in_specs=[
            SMEM,
            SMEM,
            whole(count, model),
            whole(model, rank),
            whole(rank * rank, channels),
            whole(channels, heads),
            whole(key_count, rank),
            whole(1, key_count),
            pair_spec,
        ],
        out_specs=(pair_spec, whole(key_count, lanes)),
        scratch_shapes=[
            pltpu.VMEM((count, 3 * rank, channels), F32),
            pltpu.VMEM((key_count, 3 * rank), F32),
            pltpu.VMEM((2, channels, lanes), BF16),
        ],
        name="pairs",
    )(
        chain_weight,
        query_chain,
        query_norm,
        left_proj,
        outer_proj,
        bias_proj,
        right,
        key_chain.reshape(1, key_count),
        pair_block,
    )

    part_shape = jax.ShapeDtypeStruct((count, model + 2 * LANES), F32)

    def attend_body(place, *refs):
        n = len(pieces)
        attend_kernel(place, refs[:n], *refs[n:], heads, count, None)

    part = pl.pallas_call(
        attend_body,
        out_shape=part_shape,
        in_specs=[SMEM] + [VMEM] * (len(pieces) + 3),
        out_specs=VMEM,
        name="attend",
    )(place, *pieces, half, other, bias)

    if direct:
        part = pl.pallas_call(
            functools.partial(join_kernel, heads=heads),
            out_shape=part_shape,
            in_specs=[VMEM, VMEM],
            out_specs=VMEM,
            name="join",
        )(part, exchanged(part, "col", 1))
        parts = [part] + [exchanged(part, "col", flip) for flip in (6, 4, 2)]
    else:
        parts = [lax.all_gather(part, "col")]

    def finish_body(place, *refs):
        n, k = len(pieces), len(parts)
        finish_kernel(place, refs[:n], refs[n : n + k], *refs[n + k :], heads)

    update = pl.pallas_call(
        finish_body,
        out_shape=jax.ShapeDtypeStruct((count, model), BF16),
        in_specs=[SMEM] + [VMEM] * (len(pieces) + len(parts) + 1),
        out_specs=VMEM,
        name="finish",
    )(place, *pieces, *parts, out_proj)
    return (new_pair, update.reshape(slabs, rows, model))


def solution(mesh):
    return jax.shard_map(
        on_device,
        mesh=mesh,
        in_specs=(
            P("grp", "row", "col", None),
            P("grp", "row", None),
            P(("grp", "col"), None),
            P("grp", "row"),
            P(("grp", "col")),
            P("grp", "row"),
            P(("grp", "col")),
            P("grp"),
            P(),
            P(),
            P(),
            P(),
            P(),
            P(),
            P(),
            P(None, "col"),
            P(None, "row"),
            P(),
        ),
        out_specs=(P("grp", "row", "col", None), P("grp", "row", None)),
        check_vma=False,
    )
```

```python
import functools
import math

import jax
import jax.numpy as jnp
from jax import lax
from jax.experimental import pallas as pl
from jax.experimental.pallas import tpu as pltpu
from jax.sharding import PartitionSpec as P

EPSILON = 1e-05
HIGHEST = lax.Precision.HIGHEST
LANES = 128
VMEM = pl.BlockSpec(memory_space=pltpu.VMEM)
F32 = jnp.float32
BF16 = jnp.bfloat16


def dot(left, right, precision=None):
    return jnp.dot(left, right, preferred_element_type=F32, precision=precision)


def dot_nt(left, right):
    return lax.dot_general(left, right, (((1,), (1,)), ((), ())), preferred_element_type=F32)


def dot_tn(left, right, precision=None):
    return lax.dot_general(
        left, right, (((0,), (0,)), ((), ())), preferred_element_type=F32, precision=precision
    )


def iota(shape, axis):
    return lax.broadcasted_iota(jnp.int32, shape, axis)


def split(value):
    high = value.astype(BF16)
    return high, (value - high.astype(F32)).astype(BF16)


def pick_time(step_ref, table_ref):
    table = table_ref[...].astype(F32)
    picked = iota(table.shape, 0) == step_ref[...]
    return jnp.sum(jnp.where(picked, table, 0.0), axis=0, keepdims=True)


def normalized(features, gain):
    average = jnp.mean(features, axis=-1, keepdims=True)
    centred = features - average
    spread = jnp.mean(centred * centred, axis=-1, keepdims=True)
    return (centred * lax.rsqrt(spread + EPSILON) * gain).astype(BF16)


def column_of(row):
    count = row.shape[1]
    square = (count, count)
    return jnp.sum(jnp.where(iota(square, 0) == iota(square, 1), row, 0), axis=1, keepdims=True)


def rows_column(table):
    return jnp.concatenate([column_of(table[i : i + 1]) for i in range(table.shape[0])], axis=0)


def query_kernel(step, mask, single, table, gain, proj, part_out, norm_out):
    slabs, rows, width = single.shape
    count = slabs * rows
    features = single[...].astype(F32).reshape(count, width)
    kept = rows_column(mask[...].astype(F32))
    norm = normalized(features + kept * pick_time(step, table), gain[...].reshape(1, width))
    norm_out[...] = norm
    part_out[...] = dot_nt(norm, proj[...]).astype(BF16)


def key_kernel(step, mask, single, table, gain, proj, right_proj, half_out, right_out):
    kept = column_of(mask[...].astype(F32))
    features = single[...].astype(F32) + kept * pick_time(step, table)
    norm = normalized(features, gain[...].reshape(1, features.shape[1]))
    half_out[...] = dot(norm, proj[...]).astype(BF16)
    right_out[...] = dot_nt(norm, right_proj[...])


def pair_kernel(
    chain_weight,
    query_chain,
    query_norm,
    left_proj,
    outer_proj,
    bias_proj,
    right,
    key_chain,
    pair,
    pair_out,
    bias_out,
    mixer_scratch,
    spread_scratch,
    weight_scratch,
):
    step = pl.program_id(0)
    count = query_norm.shape[0]
    rank = left_proj.shape[0]
    heads, channels = bias_proj.shape
    key_count = right.shape[0]
    lanes = heads * count
    block = pair.shape[1]

    @pl.when(step == 0)
    def _():
        left = dot_nt(query_norm[...], left_proj[...])
        repeated = (iota((rank, rank * rank), 1) // rank == iota((rank, rank * rank), 0)).astype(F32)
        wide = dot(left, repeated, HIGHEST)
        tall = jnp.broadcast_to(wide[:, None, :], (count, rank, rank * rank))
        tall = tall.reshape(count * rank, rank * rank)
        spot = (count * rank, rank * rank)
        tall = jnp.where(iota(spot, 0) % rank == iota(spot, 1) % rank, tall, 0.0)
        mixer = dot(tall, outer_proj[...].astype(F32), HIGHEST).reshape(count, rank, channels)
        high, low = split(mixer)
        mixer_scratch[:, :rank, :] = high.astype(F32)
        mixer_scratch[:, rank : 2 * rank, :] = high.astype(F32)
        mixer_scratch[:, 2 * rank :, :] = low.astype(F32)
        high, low = split(right[...])
        spread_scratch[...] = jnp.concatenate(
            [high.astype(F32), low.astype(F32), high.astype(F32)], axis=1
        )
        expand = (iota((heads, lanes), 1) // count == iota((heads, lanes), 0)).astype(F32)
        high, low = split(dot_tn(bias_proj[...], expand, HIGHEST))
        weight_scratch[0] = high
        weight_scratch[1] = low
        spot = (heads, lanes)
        weights = jnp.where(iota(spot, 1) // count == iota(spot, 0), column_of(chain_weight[...]), 0.0)
        weights = jnp.sum(weights, axis=0, keepdims=True)
        spot = (count, lanes)
        chains = rows_column(query_chain[...])
        chains = jnp.where(iota(spot, 1) % count == iota(spot, 0), chains, 0)
        chains = jnp.sum(chains, axis=0, keepdims=True)
        own = column_of(key_chain[...])
        bias_out[...] = jnp.where(own != chains, weights, 0.0)

    lane = iota((key_count, lanes), 1)
    spread = spread_scratch[...].astype(BF16)
    total = bias_out[...]
    for index in range(block):
        mixer = mixer_scratch[step * block + index].astype(BF16)
        fresh = pair[0, index] + dot(spread, mixer)
        pair_out[0, index] = fresh
        high, low = split(fresh)
        here = dot(high, weight_scratch[0]) + dot(high, weight_scratch[1]) + dot(low, weight_scratch[0])
        total = jnp.where(lane % count == step * block + index, total + here, total)
    bias_out[...] = total


def listed(refs):
    values = []
    for ref in refs:
        values += [ref[...]] if len(ref.shape) == 2 else [ref[i] for i in range(ref.shape[0])]
    return values


def gathered(pieces, col, start, stop):
    values = listed(pieces)
    if len(values) == 1:
        return values[0][:, start:stop]
    share = values[0].shape[1]
    blocks = []
    for target in range(start // share, stop // share):
        chosen = values[0]
        for index in range(1, len(values)):
            chosen = jnp.where((col ^ target) == index, values[index], chosen)
        blocks.append(chosen)
    return jnp.concatenate(blocks, axis=1)


def attend_kernel(place, pieces, own, other, bias, part_out, heads, count):
    col, row = place[0:1, 0:1], place[0:1, 1:2]
    model = own.shape[1]
    head = model // heads
    query = gathered(pieces, col, 0, model)
    first, second = own[...], other[...]
    keys = jnp.where(row == 0, first, second)
    values = jnp.where(row == 0, second, first)
    lane = iota((count, model), 1)
    spread = jnp.concatenate(
        [jnp.where(lane // head == index, query, jnp.zeros_like(query)) for index in range(heads)],
        axis=0,
    )
    scores = dot_nt(keys, spread) * (1.0 / math.sqrt(head)) + bias[...]
    peak = jnp.max(scores, axis=0, keepdims=True)
    exponent = jnp.exp(scores - peak)
    total = jnp.sum(exponent, axis=0, keepdims=True)
    summed = dot_tn(exponent.astype(BF16), values)
    lanes = heads * count
    spot = (count, lanes)
    keep = iota(spot, 1) % count == iota(spot, 0)
    gather = (iota((lanes, LANES), 0) // count == iota((lanes, LANES), 1)).astype(F32)
    stats = jnp.concatenate([jnp.where(keep, peak, 0.0), jnp.where(keep, total, 0.0)], axis=0)
    stats = dot(stats, gather, HIGHEST)
    taken = jnp.zeros((count, model), F32)
    for index in range(heads):
        taken = jnp.where(lane // head == index, summed[index * count : (index + 1) * count], taken)
    part_out[:, :model] = taken
    part_out[:, model : model + LANES] = stats[:count]
    part_out[:, model + LANES :] = stats[count:]


def merged(parts, heads):
    model = parts[0].shape[1] - 2 * LANES
    count = parts[0].shape[0]
    peak = functools.reduce(jnp.maximum, [part[:, model : model + LANES] for part in parts])
    scales = [jnp.exp(part[:, model : model + LANES] - peak) for part in parts]
    total = sum(scale * part[:, model + LANES :] for scale, part in zip(scales, parts))
    widen = (iota((LANES, model), 1) // (model // heads) == iota((LANES, model), 0)).astype(F32)
    wide = dot(jnp.concatenate(scales + [total], axis=0), widen, HIGHEST)
    summed = sum(
        wide[index * count : (index + 1) * count] * part[:, :model] for index, part in enumerate(parts)
    )
    return summed, peak, total, wide[len(parts) * count :]


def join_kernel(first, second, part_out, heads):
    summed, peak, total, _ = merged([first[...], second[...]], heads)
    model = summed.shape[1]
    part_out[:, :model] = summed
    part_out[:, model : model + LANES] = peak
    part_out[:, model + LANES :] = total


def finish_kernel(place, pieces, parts, out_proj, update_out, heads):
    col = place[0:1, 0:1]
    model = out_proj.shape[0]
    gate = gathered(pieces, col, model, 2 * model)
    values = listed(parts)
    summed, _, _, total = merged(values, heads)
    attended = (summed / total * jax.nn.sigmoid(gate.astype(F32))).astype(BF16)
    update_out[...] = dot(attended, out_proj[...]).astype(BF16)


def exchanged(value, axis, flip):
    size = lax.axis_size(axis)
    return lax.ppermute(value, axis, [(index, index ^ flip) for index in range(size)])


def on_device(
    pair_block,
    query_single,
    key_single,
    query_chain,
    key_chain,
    query_mask,
    key_mask,
    timestep,
    time_table,
    norm_gain,
    left_proj,
    right_proj,
    outer_proj,
    bias_proj,
    chain_weight,
    query_proj,
    kv_proj,
    out_proj,
):
    slabs, rows, model = query_single.shape
    count = slabs * rows
    key_count = key_single.shape[0]
    heads = chain_weight.shape[0]
    channels = pair_block.shape[-1]
    rank = left_proj.shape[1]
    lanes = heads * count
    cols = lax.axis_size("col")
    step_index = timestep.reshape(1, 1)
    place = jnp.stack([lax.axis_index("col"), lax.axis_index("row")]).astype(jnp.int32)[None]
    grant = pltpu.CompilerParams(vmem_limit_bytes=16 << 20)

    query_part, query_norm = pl.pallas_call(
        query_kernel,
        out_shape=(
            jax.ShapeDtypeStruct((count, query_proj.shape[1]), BF16),
            jax.ShapeDtypeStruct((count, model), BF16),
        ),
        in_specs=[VMEM] * 6,
        out_specs=(VMEM, VMEM),
        compiler_params=grant,
        name="query",
    )(step_index, query_mask, query_single, time_table, norm_gain, query_proj.T)

    half, right = pl.pallas_call(
        key_kernel,
        out_shape=(
            jax.ShapeDtypeStruct((key_count, kv_proj.shape[1]), BF16),
            jax.ShapeDtypeStruct((key_count, rank), F32),
        ),
        in_specs=[VMEM] * 7,
        out_specs=(VMEM, VMEM),
        compiler_params=grant,
        name="keys",
    )(
        step_index,
        key_mask.reshape(1, key_count),
        key_single,
        time_table,
        norm_gain,
        kv_proj,
        right_proj.T,
    )
    other = exchanged(half, "row", 1)

    direct = cols == 8
    if direct:
        near = exchanged(query_part, "col", 1)
        both = jnp.stack([query_part, near])
        pieces = [query_part, near]
        for flip in (2, 4, 6):
            pieces.append(exchanged(both, "col", flip))
    else:
        pieces = [lax.all_gather(query_part, "col", axis=1, tiled=True)]

    steps = 4
    block = count // steps
    per_slab = rows // block
    whole = lambda *shape: pl.BlockSpec(shape, lambda i: (0,) * len(shape))
    pair_spec = pl.BlockSpec(
        (1, block, key_count, channels), lambda i: (i // per_slab, i % per_slab, 0, 0)
    )
    new_pair, bias = pl.pallas_call(
        pair_kernel,
        grid=(steps,),
        out_shape=(
            jax.ShapeDtypeStruct(pair_block.shape, F32),
            jax.ShapeDtypeStruct((key_count, lanes), F32),
        ),
        in_specs=[
            whole(1, heads),
            whole(slabs, rows),
            whole(count, model),
            whole(rank, model),
            whole(rank * rank, channels),
            whole(heads, channels),
            whole(key_count, rank),
            whole(1, key_count),
            pair_spec,
        ],
        out_specs=(pair_spec, whole(key_count, lanes)),
        scratch_shapes=[
            pltpu.VMEM((count, 3 * rank, channels), F32),
            pltpu.VMEM((key_count, 3 * rank), F32),
            pltpu.VMEM((2, channels, lanes), BF16),
        ],
        compiler_params=grant,
        name="pairs",
    )(
        chain_weight.reshape(1, heads),
        query_chain,
        query_norm,
        left_proj.T,
        outer_proj,
        bias_proj.T,
        right,
        key_chain.reshape(1, key_count),
        pair_block,
    )

    part_shape = jax.ShapeDtypeStruct((count, model + 2 * LANES), F32)

    def attend_body(place, *refs):
        n = len(pieces)
        attend_kernel(place, refs[:n], *refs[n:], heads, count)

    part = pl.pallas_call(
        attend_body,
        out_shape=part_shape,
        in_specs=[VMEM] * (len(pieces) + 4),
        out_specs=VMEM,
        compiler_params=grant,
        name="attend",
    )(place, *pieces, half, other, bias)

    if direct:
        part = pl.pallas_call(
            functools.partial(join_kernel, heads=heads),
            out_shape=part_shape,
            in_specs=[VMEM, VMEM],
            out_specs=VMEM,
            compiler_params=grant,
            name="join",
        )(part, exchanged(part, "col", 1))
        parts = [part] + [exchanged(part, "col", flip) for flip in (6, 4, 2)]
    else:
        parts = [lax.all_gather(part, "col")]

    def finish_body(place, *refs):
        n, k = len(pieces), len(parts)
        finish_kernel(place, refs[:n], refs[n : n + k], *refs[n + k :], heads)

    update = pl.pallas_call(
        finish_body,
        out_shape=jax.ShapeDtypeStruct((count, model), BF16),
        in_specs=[VMEM] * (len(pieces) + len(parts) + 2),
        out_specs=VMEM,
        compiler_params=grant,
        name="finish",
    )(place, *pieces, *parts, out_proj)
    return (new_pair, update.reshape(slabs, rows, model))


def solution(mesh):
    return jax.shard_map(
        on_device,
        mesh=mesh,
        in_specs=(
            P("grp", "row", "col", None),
            P("grp", "row", None),
            P(("grp", "col"), None),
            P("grp", "row"),
            P(("grp", "col")),
            P("grp", "row"),
            P(("grp", "col")),
            P("grp"),
            P(),
            P(),
            P(),
            P(),
            P(),
            P(),
            P(),
            P(None, "col"),
            P(None, "row"),
            P(),
        ),
        out_specs=(P("grp", "row", "col", None), P("grp", "row", None)),
        check_vma=False,
    )
```

```python
import functools
import math

import jax
import jax.numpy as jnp
from jax import lax
from jax.experimental import pallas as pl
from jax.experimental.pallas import tpu as pltpu
from jax.sharding import PartitionSpec as P


EPSILON = 1e-05
HIGHEST = lax.Precision.HIGHEST
LANES = 128
TERM = LANES // 5
VMEM = pl.BlockSpec(memory_space=pltpu.VMEM)
HBM = pl.BlockSpec(memory_space=pltpu.HBM)
SMEM = pl.BlockSpec(memory_space=pltpu.SMEM)
F32 = jnp.float32
BF16 = jnp.bfloat16


def dot(left, right, precision=None):
    return jnp.dot(left, right, preferred_element_type=F32, precision=precision)


def dot_nt(left, right):
    return lax.dot_general(left, right, (((1,), (1,)), ((), ())), preferred_element_type=F32)


def dot_tn(left, right, precision=None):
    return lax.dot_general(
        left, right, (((0,), (0,)), ((), ())), preferred_element_type=F32, precision=precision
    )


def iota(shape, axis):
    return lax.broadcasted_iota(jnp.int32, shape, axis)


def split(value):
    high = value.astype(BF16)
    return high, (value - high.astype(F32)).astype(BF16)


def normalized(features, gain):
    average = jnp.mean(features, axis=-1, keepdims=True)
    centred = features - average
    spread = jnp.mean(centred * centred, axis=-1, keepdims=True)
    return (centred * lax.rsqrt(spread + EPSILON) * gain).astype(BF16)


def column_of(row):
    count = row.shape[1]
    square = (count, count)
    return jnp.sum(jnp.where(iota(square, 0) == iota(square, 1), row, 0), axis=1, keepdims=True)


def rows_column(table):
    return jnp.concatenate([column_of(table[i : i + 1]) for i in range(table.shape[0])], axis=0)


def query_kernel(*refs):
    step, mask, single, table, gain, proj = refs[:6]
    later = refs[6:10]
    part_out, norm_out, time_out, gain_out = refs[10:14]
    later_out = refs[14:18]
    mask_in, single_in, table_in, proj_in, sems = refs[18:]
    sources = (mask, single, table, gain, proj) + later
    targets = (mask_in, single_in, table_in, gain_out, proj_in) + later_out
    copies = [
        pltpu.make_async_copy(source, target, sems.at[index])
        for index, (source, target) in enumerate(zip(sources, targets))
    ]
    for copy in copies:
        copy.start()
    for copy in copies[:4]:
        copy.wait()
    slabs, rows, width = single.shape
    features = single_in[...].astype(F32).reshape(slabs * rows, width)
    kept = rows_column(mask_in[...].astype(F32))
    held = table_in[...].astype(F32)
    time_row = jnp.sum(jnp.where(iota(held.shape, 0) == step[0], held, 0.0), axis=0, keepdims=True)
    time_out[...] = time_row
    norm = normalized(features + kept * time_row, gain_out[...].reshape(1, width))
    norm_out[...] = norm
    copies[4].wait()
    part_out[...] = dot_nt(norm, proj_in[...]).astype(BF16)
    for copy in copies[5:]:
        copy.wait()


def key_kernel(time_row, gain, single, proj, mask, right_proj, half_out, right_out):
    kept = column_of(mask[...].astype(F32))
    features = single[...].astype(F32) + kept * time_row[...]
    norm = normalized(features, gain[...].reshape(1, features.shape[1]))
    half_out[...] = dot(norm, proj[...]).astype(BF16)
    right_out[...] = dot_nt(norm, right_proj[...])


def pair_kernel(
    chain_weight,
    query_chain,
    query_norm,
    left_proj,
    outer_proj,
    bias_proj,
    right,
    key_chain,
    pair,
    pair_out,
    bias_out,
    fresh_scratch,
    sems,
):
    slabs, rows = query_chain.shape
    count = slabs * rows
    rank = left_proj.shape[0]
    heads, channels = bias_proj.shape
    key_count = right.shape[0]
    lanes = heads * count
    left = dot_nt(query_norm[...], left_proj[...])
    spot = (rank, rank * rank)
    wide = dot(left, (iota(spot, 1) // rank == iota(spot, 0)).astype(F32), HIGHEST)
    tall = jnp.broadcast_to(wide[:, None, :], (count, rank, rank * rank))
    tall = tall.reshape(count * rank, rank * rank)
    spot = (count * rank, rank * rank)
    tall = jnp.where(iota(spot, 0) % rank == iota(spot, 1) % rank, tall, 0.0)
    mixer = dot(tall, outer_proj[...].astype(F32), HIGHEST).reshape(count, rank, channels)
    high, low = (part.astype(F32) for part in split(mixer))
    mixer = jnp.concatenate([high, high, low], axis=1).astype(BF16)
    high, low = (part.astype(F32) for part in split(right[...]))
    spread = jnp.concatenate([high, low, high], axis=1).astype(BF16)
    spot = (heads, lanes)
    expand = iota(spot, 1) // count == iota(spot, 0)
    high, low = split(dot_tn(bias_proj[...], expand.astype(F32), HIGHEST))
    weights = jnp.concatenate([high, high, low], axis=0)
    apart = jnp.sum(jnp.where(expand, column_of(chain_weight[...]), 0.0), axis=0, keepdims=True)
    spot = (count, lanes)
    chains = jnp.where(iota(spot, 1) % count == iota(spot, 0), rows_column(query_chain[...]), 0)
    chains = jnp.sum(chains, axis=0, keepdims=True)
    total = jnp.where(column_of(key_chain[...]) != chains, apart, 0.0)
    lane = iota((key_count, lanes), 1) % count
    bias = jnp.zeros((key_count, lanes), F32)
    copies = []
    for index in range(count):
        spot = (index // rows, index % rows)
        fresh = pair[spot] + dot(spread, mixer[index])
        fresh_scratch[index] = fresh
        copy = pltpu.make_async_copy(fresh_scratch.at[index], pair_out.at[spot], sems.at[index])
        copy.start()
        copies.append(copy)
        high, low = split(fresh)
        here = dot(jnp.concatenate([high, low, high], axis=1), weights)
        bias = jnp.where(lane == index, here, bias)
    bias_out[...] = bias + total
    for copy in copies:
        copy.wait()


def listed(refs):
    values = []
    for ref in refs:
        values += [ref[...]] if len(ref.shape) == 2 else [ref[i] for i in range(ref.shape[0])]
    return values


def gathered(pieces, col, start, stop):
    values = listed(pieces)
    if len(values) == 1:
        return values[0][:, start:stop]
    share = values[0].shape[1]
    blocks = []
    for target in range(start // share, stop // share):
        chosen = values[0]
        for index in range(1, len(values)):
            chosen = jnp.where((col ^ target) == index, values[index], chosen)
        blocks.append(chosen)
    return jnp.concatenate(blocks, axis=1)


def attend_kernel(pieces, halves, biases, part_out, heads, count):
    col, row = lax.axis_index("col"), lax.axis_index("row")
    model = halves[0].shape[1]
    head = model // heads
    lanes = heads * count
    query = gathered(pieces, col, 0, model)
    firsts = [ref[...] for ref in halves[::2]]
    seconds = [ref[...] for ref in halves[1::2]]
    keys = [jnp.where(row == 0, first, second) for first, second in zip(firsts, seconds)]
    values = [jnp.where(row == 0, second, first) for first, second in zip(firsts, seconds)]
    lane = iota((count, model), 1)
    spread = jnp.concatenate(
        [jnp.where(lane // head == index, query, jnp.zeros_like(query)) for index in range(heads)],
        axis=0,
    )
    scale = 1.0 / math.sqrt(head)
    scores = [dot_nt(key, spread) * scale + bias[...] for key, bias in zip(keys, biases)]
    peak = functools.reduce(jnp.maximum, [jnp.max(score, axis=0, keepdims=True) for score in scores])
    exponents = [jnp.exp(score - peak) for score in scores]
    total = sum(jnp.sum(exponent, axis=0, keepdims=True) for exponent in exponents)
    weights = jnp.concatenate([exponent.astype(BF16) for exponent in exponents], axis=0)
    summed = dot_tn(weights, jnp.concatenate(values, axis=0))
    taken = jnp.zeros((count, model), F32)
    for index in range(heads):
        taken = jnp.where(lane // head == index, summed[index * count : (index + 1) * count], taken)
    part_out[:, :model] = taken.astype(BF16)
    spot = (count, lanes)
    keep = iota(spot, 1) % count == iota(spot, 0)
    terms = terms_of(peak, 3) + terms_of(total, 2)
    rows = jnp.concatenate([jnp.where(keep, term, 0.0).astype(BF16) for term in terms], axis=1)
    spot = (len(terms) * lanes, LANES)
    source = iota(spot, 0)
    target = source // lanes * TERM + source % lanes // count
    part_out[:, model:] = dot(rows, (target == iota(spot, 1)).astype(BF16)).astype(BF16)


def terms_of(value, count):
    terms = []
    for _ in range(count):
        term = value.astype(BF16).astype(F32)
        terms.append(term)
        value = value - term
    return terms


def merged(parts, heads):
    model = parts[0].shape[1] - LANES
    count = parts[0].shape[0]
    spot = (LANES, model)
    term, place = iota(spot, 0), iota(spot, 1) // (model // heads)
    ours = term % TERM == place
    for_peak = (ours & (term // TERM < 3)).astype(BF16)
    for_total = (ours & (term // TERM >= 3) & (term // TERM < 5)).astype(BF16)
    stats = jnp.concatenate([part[:, model:] for part in parts], axis=0)
    peaks, totals = dot(stats, for_peak), dot(stats, for_total)
    cut = lambda array, index: array[index * count : (index + 1) * count]
    peak = functools.reduce(jnp.maximum, [cut(peaks, index) for index in range(len(parts))])
    scales = [jnp.exp(cut(peaks, index) - peak) for index in range(len(parts))]
    total = sum(scale * cut(totals, index) for index, scale in enumerate(scales))
    summed = sum(scale * part[:, :model].astype(F32) for scale, part in zip(scales, parts))
    return summed / total


def finish_kernel(pieces, parts, out_proj, update_out, heads):
    model = out_proj.shape[0]
    gate = gathered(pieces, lax.axis_index("col"), model, 2 * model)
    average = merged(listed(parts), heads)
    attended = (average * jax.nn.sigmoid(gate.astype(F32))).astype(BF16)
    update_out[...] = dot(attended, out_proj[...]).astype(BF16)


def exchanged(value, axis, flip):
    size = lax.axis_size(axis)
    return lax.ppermute(value, axis, [(index, index ^ flip) for index in range(size)])


def on_device(
    pair_block,
    query_single,
    key_single,
    query_chain,
    key_chain,
    query_mask,
    key_mask,
    timestep,
    time_table,
    norm_gain,
    left_proj,
    right_proj,
    outer_proj,
    bias_proj,
    chain_weight,
    query_proj,
    kv_proj,
    out_proj,
):
    slabs, rows, model = query_single.shape
    count = slabs * rows
    key_count = key_single.shape[0]
    heads = chain_weight.shape[0]
    channels = pair_block.shape[-1]
    rank = left_proj.shape[1]
    lanes = heads * count
    cols = lax.axis_size("col")
    direct = cols == 8
    grant = pltpu.CompilerParams(vmem_limit_bytes=16 << 20)
    now = (query_mask, query_single, time_table, norm_gain, query_proj.T)
    later = (key_single, kv_proj, key_mask.reshape(1, key_count), right_proj.T)
    shape_of = lambda array: jax.ShapeDtypeStruct(array.shape, array.dtype)
    scratch_of = lambda array: pltpu.VMEM(array.shape, array.dtype)

    query_part, query_norm, time_row, gain, *later = pl.pallas_call(
        query_kernel,
        out_shape=(
            jax.ShapeDtypeStruct((count, query_proj.shape[1]), BF16),
            jax.ShapeDtypeStruct((count, model), BF16),
            jax.ShapeDtypeStruct((1, model), F32),
            shape_of(norm_gain),
        )
        + tuple(shape_of(array) for array in later),
        in_specs=[SMEM] + [HBM] * 9,
        out_specs=[VMEM] * 8,
        scratch_shapes=[
            scratch_of(query_mask),
            scratch_of(query_single),
            scratch_of(time_table),
            scratch_of(query_proj.T),
            pltpu.SemaphoreType.DMA((9,)),
        ],
        compiler_params=grant,
        name="query",
    )(timestep, *[pltpu.with_memory_space_constraint(array, pltpu.HBM) for array in now + later])

    if direct:
        near = exchanged(query_part, "col", 1)

    half, right = pl.pallas_call(
        key_kernel,
        out_shape=(
            jax.ShapeDtypeStruct((key_count, kv_proj.shape[1]), BF16),
            jax.ShapeDtypeStruct((key_count, rank), F32),
        ),
        in_specs=[VMEM] * 6,
        out_specs=(VMEM, VMEM),
        compiler_params=grant,
        name="keys",
    )(time_row, gain, *later)
    halves = [half, exchanged(half, "row", 1)]
    if direct:
        far = exchanged(half, "col", 1)
        halves += [far, exchanged(far, "row", 1)]

    new_pair, bias = pl.pallas_call(
        pair_kernel,
        out_shape=(
            jax.ShapeDtypeStruct(pair_block.shape, F32),
            jax.ShapeDtypeStruct((key_count, lanes), F32),
        ),
        in_specs=[VMEM] * 9,
        out_specs=(HBM, VMEM),
        scratch_shapes=[
            pltpu.VMEM((count, key_count, channels), F32),
            pltpu.SemaphoreType.DMA((count,)),
        ],
        compiler_params=grant,
        name="pairs",
    )(
        chain_weight.reshape(1, heads),
        query_chain,
        query_norm,
        left_proj.T,
        outer_proj,
        bias_proj.T,
        right,
        key_chain.reshape(1, key_count),
        pair_block,
    )
    biases = [bias]

    if direct:
        both = jnp.stack([query_part, near])
        both, bias = lax.optimization_barrier((both, bias))
        biases = [bias, exchanged(bias, "col", 1)]
        pieces = [query_part, near] + [exchanged(both, "col", flip) for flip in (2, 4, 6)]
    else:
        pieces = [lax.all_gather(query_part, "col", axis=1, tiled=True)]

    def attend_body(*refs):
        n, k = len(pieces), len(halves)
        attend_kernel(refs[:n], refs[n : n + k], refs[n + k : -1], refs[-1], heads, count)

    part = pl.pallas_call(
        attend_body,
        out_shape=jax.ShapeDtypeStruct((count, model + LANES), BF16),
        in_specs=[VMEM] * (len(pieces) + len(halves) + len(biases)),
        out_specs=VMEM,
        compiler_params=grant,
        name="attend",
    )(*pieces, *halves, *biases)

    if direct:
        parts = [part] + [exchanged(part, "col", flip) for flip in (2, 4, 6)]
    else:
        parts = [lax.all_gather(part, "col")]

    def finish_body(*refs):
        n, k = len(pieces), len(parts)
        finish_kernel(refs[:n], refs[n : n + k], *refs[n + k :], heads)

    update = pl.pallas_call(
        finish_body,
        out_shape=jax.ShapeDtypeStruct((count, model), BF16),
        in_specs=[VMEM] * (len(pieces) + len(parts) + 1),
        out_specs=VMEM,
        compiler_params=grant,
        name="finish",
    )(*pieces, *parts, out_proj)
    return (new_pair, update.reshape(slabs, rows, model))


def solution(mesh):
    return jax.shard_map(
        on_device,
        mesh=mesh,
        in_specs=(
            P("grp", "row", "col", None),
            P("grp", "row", None),
            P(("grp", "col"), None),
            P("grp", "row"),
            P(("grp", "col")),
            P("grp", "row"),
            P(("grp", "col")),
            P("grp"),
            P(),
            P(),
            P(),
            P(),
            P(),
            P(),
            P(),
            P(None, "col"),
            P(None, "row"),
            P(),
        ),
        out_specs=(P("grp", "row", "col", None), P("grp", "row", None)),
        check_vma=False,
    )
```

```python
import functools
import math

import jax
import jax.numpy as jnp
from jax import lax
from jax.experimental import pallas as pl
from jax.experimental.pallas import tpu as pltpu
from jax.sharding import PartitionSpec as P


EPSILON = 1e-05
HIGHEST = lax.Precision.HIGHEST
LANES = 128
TERM = LANES // 5
GROUP = 4
VMEM = pl.BlockSpec(memory_space=pltpu.VMEM)
HBM = pl.BlockSpec(memory_space=pltpu.HBM)
SMEM = pl.BlockSpec(memory_space=pltpu.SMEM)
F32 = jnp.float32
BF16 = jnp.bfloat16


def dot(left, right, precision=None):
    return jnp.dot(left, right, preferred_element_type=F32, precision=precision)


def dot_nt(left, right):
    return lax.dot_general(left, right, (((1,), (1,)), ((), ())), preferred_element_type=F32)


def dot_tn(left, right, precision=None):
    return lax.dot_general(
        left, right, (((0,), (0,)), ((), ())), preferred_element_type=F32, precision=precision
    )


def iota(shape, axis):
    return lax.broadcasted_iota(jnp.int32, shape, axis)


def split(value):
    high = value.astype(BF16)
    return high, (value - high.astype(F32)).astype(BF16)


def normalized(features, gain):
    average = jnp.mean(features, axis=-1, keepdims=True)
    centred = features - average
    spread = jnp.mean(centred * centred, axis=-1, keepdims=True)
    return (centred * lax.rsqrt(spread + EPSILON) * gain).astype(BF16)


def column_of(row):
    count = row.shape[1]
    square = (count, count)
    return jnp.sum(jnp.where(iota(square, 0) == iota(square, 1), row, 0), axis=1, keepdims=True)


def rows_column(table):
    return jnp.concatenate([column_of(table[i : i + 1]) for i in range(table.shape[0])], axis=0)


def query_kernel(*refs):
    step, mask, single, table, gain, proj = refs[:6]
    later = refs[6:10]
    part_out, norm_out, time_out, gain_out = refs[10:14]
    later_out = refs[14:18]
    mask_in, single_in, table_in, proj_in, sems = refs[18:]
    sources = (mask, single, table, gain, proj) + later
    targets = (mask_in, single_in, table_in, gain_out, proj_in) + later_out
    copies = [
        pltpu.make_async_copy(source, target, sems.at[index])
        for index, (source, target) in enumerate(zip(sources, targets))
    ]
    for copy in copies:
        copy.start()
    for copy in copies[:4]:
        copy.wait()
    slabs, rows, width = single.shape
    features = single_in[...].astype(F32).reshape(slabs * rows, width)
    kept = rows_column(mask_in[...].astype(F32))
    held = table_in[...].astype(F32)
    time_row = jnp.sum(jnp.where(iota(held.shape, 0) == step[0], held, 0.0), axis=0, keepdims=True)
    time_out[...] = time_row
    norm = normalized(features + kept * time_row, gain_out[...].reshape(1, width))
    norm_out[...] = norm
    copies[4].wait()
    part_out[...] = dot_nt(norm, proj_in[...]).astype(BF16)
    for copy in copies[5:]:
        copy.wait()


def key_kernel(time_row, gain, single, proj, mask, right_proj, half_out, right_out):
    kept = column_of(mask[...].astype(F32))
    features = single[...].astype(F32) + kept * time_row[...]
    norm = normalized(features, gain[...].reshape(1, features.shape[1]))
    half_out[...] = dot(norm, proj[...]).astype(BF16)
    right_out[...] = dot_nt(norm, right_proj[...])


def pair_kernel(
    chain_weight,
    query_chain,
    query_norm,
    left_proj,
    outer_proj,
    bias_proj,
    right,
    key_chain,
    pair,
    pair_out,
    bias_out,
    terms_out,
    fresh_scratch,
    sems,
):
    slabs, rows = query_chain.shape
    count = slabs * rows
    rank = left_proj.shape[0]
    heads, channels = bias_proj.shape
    key_count = right.shape[0]
    lanes = heads * count
    left = dot_nt(query_norm[...], left_proj[...])
    spot = (rank, rank * rank)
    wide = dot(left, (iota(spot, 1) // rank == iota(spot, 0)).astype(F32), HIGHEST)
    tall = jnp.broadcast_to(wide[:, None, :], (count, rank, rank * rank))
    tall = tall.reshape(count * rank, rank * rank)
    spot = (count * rank, rank * rank)
    tall = jnp.where(iota(spot, 0) % rank == iota(spot, 1) % rank, tall, 0.0)
    mixer = dot(tall, outer_proj[...].astype(F32), HIGHEST).reshape(count, rank, channels)
    high, low = (part.astype(F32) for part in split(mixer))
    mixer = jnp.concatenate([high, high, low, jnp.zeros_like(low)], axis=1).astype(BF16)
    high, low = (part.astype(F32) for part in split(right[...]))
    spread = jnp.concatenate([high, low, high, jnp.zeros_like(low)], axis=1).astype(BF16)
    head_of = iota((1, lanes), 1) // count
    row_of = iota((1, lanes), 1) - head_of * count
    expand = head_of == iota((heads, lanes), 0)
    high, low = split(dot_tn(bias_proj[...], expand.astype(F32), HIGHEST))
    weights = jnp.concatenate([high, high, low], axis=0)
    apart = jnp.sum(jnp.where(expand, column_of(chain_weight[...]), 0.0), axis=0, keepdims=True)
    chains = jnp.where(row_of == iota((count, lanes), 0), rows_column(query_chain[...]), 0)
    chains = jnp.sum(chains, axis=0, keepdims=True)
    bias = jnp.zeros((key_count, lanes), F32)
    copies = []
    for start in range(0, count, GROUP):
        indices = range(start, start + GROUP)
        updates = dot(spread, jnp.concatenate([mixer[index] for index in indices], axis=1))
        terms = []
        for index in indices:
            spot = (index // rows, index % rows)
            place = (index - start) * channels
            fresh = pair[spot] + updates[:, place : place + channels]
            fresh_scratch[index] = fresh
            copy = pltpu.make_async_copy(fresh_scratch.at[index], pair_out.at[spot], sems.at[index])
            copy.start()
            copies.append(copy)
            high, low = split(fresh)
            terms.append(jnp.concatenate([high, low, high], axis=1))
        here = dot(jnp.concatenate(terms, axis=0), weights)
        for index in indices:
            place = (index - start) * key_count
            bias = jnp.where(row_of == index, here[place : place + key_count], bias)
    bias = bias + jnp.where(column_of(key_chain[...]) != chains, apart, 0.0)
    bias_out[...] = bias
    high, low = split(bias)
    terms_out[:key_count] = high
    terms_out[key_count:] = low
    for copy in copies:
        copy.wait()


def listed(refs):
    values = []
    for ref in refs:
        values += [ref[...]] if len(ref.shape) == 2 else [ref[i] for i in range(ref.shape[0])]
    return values


def gathered(pieces, start, stop):
    if len(pieces) == 1:
        return pieces[0][:, start:stop]
    col = lax.axis_index("col")
    ours = listed(pieces[:3])
    count, share = ours[0].shape
    message = pieces[3]
    base = message.shape[0] - len(ours) * count
    values = []
    for index, value in enumerate(ours):
        values += [value, message[base + index * count : base + (index + 1) * count]]
    blocks = []
    for target in range(start // share, stop // share):
        chosen = values[0]
        for index in range(1, len(values)):
            chosen = jnp.where((col ^ target) == index, values[index], chosen)
        blocks.append(chosen)
    return jnp.concatenate(blocks, axis=1)


def attend_kernel(pieces, halves, bias_ref, part_out, heads, count):
    row = lax.axis_index("row")
    key_count, model = halves[0].shape
    head = model // heads
    lanes = heads * count
    query = gathered(pieces, 0, model)
    biases = [bias_ref[...]]
    if len(pieces) > 1:
        message = pieces[3]
        biases.append(
            message[:key_count].astype(F32) + message[key_count : 2 * key_count].astype(F32)
        )
    firsts = [ref[...] for ref in halves[::2]]
    seconds = [ref[...] for ref in halves[1::2]]
    keys = [jnp.where(row == 0, first, second) for first, second in zip(firsts, seconds)]
    values = [jnp.where(row == 0, second, first) for first, second in zip(firsts, seconds)]
    head_of = iota((1, model), 1) // head
    spread = jnp.concatenate(
        [jnp.where(head_of == index, query, jnp.zeros_like(query)) for index in range(heads)],
        axis=0,
    )
    scale = 1.0 / math.sqrt(head)
    scores = [dot_nt(key, spread) * scale + bias for key, bias in zip(keys, biases)]
    peak = functools.reduce(jnp.maximum, [jnp.max(score, axis=0, keepdims=True) for score in scores])
    exponents = [jnp.exp(score - peak) for score in scores]
    total = sum(jnp.sum(exponent, axis=0, keepdims=True) for exponent in exponents)
    weights = jnp.concatenate([exponent.astype(BF16) for exponent in exponents], axis=0)
    summed = dot_tn(weights, jnp.concatenate(values, axis=0))
    taken = summed[:count]
    for index in range(1, heads):
        taken = jnp.where(head_of == index, summed[index * count : (index + 1) * count], taken)
    part_out[:, :model] = taken.astype(BF16)
    row_of = iota((1, lanes), 1) % count
    keep = row_of == iota((count, lanes), 0)
    source = iota((lanes, 1), 0) // count
    stats = jnp.zeros((count, LANES), F32)
    for index, term in enumerate(terms_of(peak, 3) + terms_of(total, 2)):
        target = (source + index * TERM == iota((lanes, LANES), 1)).astype(BF16)
        stats = stats + dot(jnp.where(keep, term, 0.0).astype(BF16), target)
    part_out[:, model:] = stats.astype(BF16)


def terms_of(value, count):
    terms = []
    for _ in range(count):
        term = value.astype(BF16).astype(F32)
        terms.append(term)
        value = value - term
    return terms


def merged(parts, heads):
    model = parts[0].shape[1] - LANES
    count = parts[0].shape[0]
    term = iota((LANES, 1), 0)
    place = iota((1, model), 1) // (model // heads)
    kind = term // TERM
    wanted = term - kind * TERM
    for_peak = (jnp.where(kind < 3, wanted, -1) == place).astype(BF16)
    for_total = (jnp.where((kind >= 3) & (kind < 5), wanted, -1) == place).astype(BF16)
    stats = jnp.concatenate([part[:, model:] for part in parts], axis=0)
    peaks, totals = dot(stats, for_peak), dot(stats, for_total)
    cut = lambda array, index: array[index * count : (index + 1) * count]
    peak = tree(jnp.maximum, [cut(peaks, index) for index in range(len(parts))])
    scales = [jnp.exp(cut(peaks, index) - peak) for index in range(len(parts))]
    total = tree(jnp.add, [scale * cut(totals, index) for index, scale in enumerate(scales)])
    summed = tree(jnp.add, [scale * part[:, :model].astype(F32) for scale, part in zip(scales, parts)])
    return summed / total


def tree(combine, values):
    while len(values) > 1:
        values = [
            combine(*values[index : index + 2]) if index + 1 < len(values) else values[index]
            for index in range(0, len(values), 2)
        ]
    return values[0]


def gate_kernel(*refs):
    pieces, gate_out = refs[:-1], refs[-1]
    model = gate_out.shape[1]
    gate_out[...] = jax.nn.sigmoid(gathered(pieces, model, 2 * model).astype(F32))


def finish_kernel(gate, parts, out_proj, update_out, heads):
    attended = (merged(listed(parts), heads) * gate[...]).astype(BF16)
    update_out[...] = dot(attended, out_proj[...]).astype(BF16)


def exchanged(value, axis, flip):
    size = lax.axis_size(axis)
    return lax.ppermute(value, axis, [(index, index ^ flip) for index in range(size)])


def on_device(
    pair_block,
    query_single,
    key_single,
    query_chain,
    key_chain,
    query_mask,
    key_mask,
    timestep,
    time_table,
    norm_gain,
    left_proj,
    right_proj,
    outer_proj,
    bias_proj,
    chain_weight,
    query_proj,
    kv_proj,
    out_proj,
):
    slabs, rows, model = query_single.shape
    count = slabs * rows
    key_count = key_single.shape[0]
    heads = chain_weight.shape[0]
    channels = pair_block.shape[-1]
    rank = left_proj.shape[1]
    lanes = heads * count
    cols = lax.axis_size("col")
    direct = cols == 8
    grant = pltpu.CompilerParams(vmem_limit_bytes=16 << 20)
    now = (query_mask, query_single, time_table, norm_gain, query_proj.T)
    later = (key_single, kv_proj, key_mask.reshape(1, key_count), right_proj.T)
    shape_of = lambda array: jax.ShapeDtypeStruct(array.shape, array.dtype)
    scratch_of = lambda array: pltpu.VMEM(array.shape, array.dtype)

    query_part, query_norm, time_row, gain, *later = pl.pallas_call(
        query_kernel,
        out_shape=(
            jax.ShapeDtypeStruct((count, query_proj.shape[1]), BF16),
            jax.ShapeDtypeStruct((count, model), BF16),
            jax.ShapeDtypeStruct((1, model), F32),
            shape_of(norm_gain),
        )
        + tuple(shape_of(array) for array in later),
        in_specs=[SMEM] + [HBM] * 9,
        out_specs=[VMEM] * 8,
        scratch_shapes=[
            scratch_of(query_mask),
            scratch_of(query_single),
            scratch_of(time_table),
            scratch_of(query_proj.T),
            pltpu.SemaphoreType.DMA((9,)),
        ],
        compiler_params=grant,
        name="query",
    )(timestep, *[pltpu.with_memory_space_constraint(array, pltpu.HBM) for array in now + later])

    if direct:
        beside = exchanged(query_part, "col", 2)

    half, right = pl.pallas_call(
        key_kernel,
        out_shape=(
            jax.ShapeDtypeStruct((key_count, kv_proj.shape[1]), BF16),
            jax.ShapeDtypeStruct((key_count, rank), F32),
        ),
        in_specs=[VMEM] * 6,
        out_specs=(VMEM, VMEM),
        compiler_params=grant,
        name="keys",
    )(time_row, gain, *later)
    halves = [half, exchanged(half, "row", 1)]
    if direct:
        far = exchanged(half, "col", 1)
        halves += [far, exchanged(far, "row", 1)]

    new_pair, bias, terms = pl.pallas_call(
        pair_kernel,
        out_shape=(
            jax.ShapeDtypeStruct(pair_block.shape, F32),
            jax.ShapeDtypeStruct((key_count, lanes), F32),
            jax.ShapeDtypeStruct((2 * key_count, lanes), BF16),
        ),
        in_specs=[VMEM] * 9,
        out_specs=(HBM, VMEM, VMEM),
        scratch_shapes=[
            pltpu.VMEM((count, key_count, channels), F32),
            pltpu.SemaphoreType.DMA((count,)),
        ],
        compiler_params=grant,
        name="pairs",
    )(
        chain_weight.reshape(1, heads),
        query_chain,
        query_norm,
        left_proj.T,
        outer_proj,
        bias_proj.T,
        right,
        key_chain.reshape(1, key_count),
        pair_block,
    )
    if direct:
        far = exchanged(jnp.stack([query_part, beside]), "col", 4)
        message = jnp.concatenate([terms, query_part, beside, far[0], far[1]], axis=0)
        pieces = [query_part, beside, far, exchanged(message, "col", 1)]
    else:
        pieces = [lax.all_gather(query_part, "col", axis=1, tiled=True)]

    def attend_body(*refs):
        n = len(pieces)
        attend_kernel(refs[:n], refs[n:-2], *refs[-2:], heads, count)

    part = pl.pallas_call(
        attend_body,
        out_shape=jax.ShapeDtypeStruct((count, model + LANES), BF16),
        in_specs=[VMEM] * (len(pieces) + len(halves) + 1),
        out_specs=VMEM,
        compiler_params=grant,
        name="attend",
    )(*pieces, *halves, bias)

    if direct:
        parts = [part] + [exchanged(part, "col", flip) for flip in (2, 4, 6)]
    else:
        parts = [lax.all_gather(part, "col")]

    gate = pl.pallas_call(
        gate_kernel,
        out_shape=jax.ShapeDtypeStruct((count, model), F32),
        in_specs=[VMEM] * len(pieces),
        out_specs=VMEM,
        compiler_params=grant,
        name="gate",
    )(*pieces)

    def finish_body(gate, *refs):
        finish_kernel(gate, refs[:-2], *refs[-2:], heads)

    update = pl.pallas_call(
        finish_body,
        out_shape=jax.ShapeDtypeStruct((count, model), BF16),
        in_specs=[VMEM] * (len(parts) + 2),
        out_specs=VMEM,
        compiler_params=grant,
        name="finish",
    )(gate, *parts, out_proj)
    return (new_pair, update.reshape(slabs, rows, model))


def solution(mesh):
    return jax.shard_map(
        on_device,
        mesh=mesh,
        in_specs=(
            P("grp", "row", "col", None),
            P("grp", "row", None),
            P(("grp", "col"), None),
            P("grp", "row"),
            P(("grp", "col")),
            P("grp", "row"),
            P(("grp", "col")),
            P("grp"),
            P(),
            P(),
            P(),
            P(),
            P(),
            P(),
            P(),
            P(None, "col"),
            P(None, "row"),
            P(),
        ),
        out_specs=(P("grp", "row", "col", None), P("grp", "row", None)),
        check_vma=False,
    )
```

```python
import functools
import math

import jax
import jax.numpy as jnp
from jax import lax
from jax.experimental import pallas as pl
from jax.experimental.pallas import tpu as pltpu
from jax.sharding import PartitionSpec as P


EPSILON = 1e-05
HIGHEST = lax.Precision.HIGHEST
LANES = 128
TERM = LANES // 5
GROUP = 4
VMEM = pl.BlockSpec(memory_space=pltpu.VMEM)
HBM = pl.BlockSpec(memory_space=pltpu.HBM)
SMEM = pl.BlockSpec(memory_space=pltpu.SMEM)
F32 = jnp.float32
BF16 = jnp.bfloat16


def dot(left, right, precision=None):
    return jnp.dot(left, right, preferred_element_type=F32, precision=precision)


def dot_nt(left, right):
    return lax.dot_general(left, right, (((1,), (1,)), ((), ())), preferred_element_type=F32)


def dot_tn(left, right, precision=None):
    return lax.dot_general(
        left, right, (((0,), (0,)), ((), ())), preferred_element_type=F32, precision=precision
    )


def iota(shape, axis):
    return lax.broadcasted_iota(jnp.int32, shape, axis)


def split(value):
    high = value.astype(BF16)
    return high, (value - high.astype(F32)).astype(BF16)


def normalized(features, gain):
    average = jnp.mean(features, axis=-1, keepdims=True)
    centred = features - average
    spread = jnp.mean(centred * centred, axis=-1, keepdims=True)
    return (centred * lax.rsqrt(spread + EPSILON) * gain).astype(BF16)


def column_of(row):
    count = row.shape[1]
    square = (count, count)
    return jnp.sum(jnp.where(iota(square, 0) == iota(square, 1), row, 0), axis=1, keepdims=True)


def rows_column(table):
    return jnp.concatenate([column_of(table[i : i + 1]) for i in range(table.shape[0])], axis=0)


def query_kernel(*refs):
    step, mask, single, table, gain, proj = refs[:6]
    later = refs[6:10]
    part_out, norm_out, time_out, gain_out = refs[10:14]
    later_out = refs[14:18]
    mask_in, single_in, table_in, proj_in, sems = refs[18:]
    sources = (mask, single, table, gain, proj) + later
    targets = (mask_in, single_in, table_in, gain_out, proj_in) + later_out
    copies = [
        pltpu.make_async_copy(source, target, sems.at[index])
        for index, (source, target) in enumerate(zip(sources, targets))
    ]
    for copy in copies:
        copy.start()
    for copy in copies[:4]:
        copy.wait()
    slabs, rows, width = single.shape
    features = single_in[...].astype(F32).reshape(slabs * rows, width)
    kept = rows_column(mask_in[...].astype(F32))
    held = table_in[...].astype(F32)
    time_row = jnp.sum(jnp.where(iota(held.shape, 0) == step[0], held, 0.0), axis=0, keepdims=True)
    time_out[...] = time_row
    norm = normalized(features + kept * time_row, gain_out[...].reshape(1, width))
    norm_out[...] = norm
    copies[4].wait()
    part_out[...] = dot_nt(norm, proj_in[...]).astype(BF16)
    for copy in copies[5:]:
        copy.wait()


def key_kernel(time_row, gain, single, proj, mask, right_proj, half_out, right_out):
    kept = column_of(mask[...].astype(F32))
    features = single[...].astype(F32) + kept * time_row[...]
    norm = normalized(features, gain[...].reshape(1, features.shape[1]))
    half_out[...] = dot(norm, proj[...]).astype(BF16)
    right_out[...] = dot_nt(norm, right_proj[...])


def pair_kernel(
    chain_weight,
    query_chain,
    query_norm,
    left_proj,
    outer_proj,
    bias_proj,
    right,
    key_chain,
    pair,
    pair_out,
    terms_out,
    fresh_scratch,
    sems,
):
    slabs, rows = query_chain.shape
    count = slabs * rows
    rank = left_proj.shape[0]
    heads, channels = bias_proj.shape
    key_count = right.shape[0]
    lanes = heads * count
    left = dot_nt(query_norm[...], left_proj[...])
    spot = (rank, rank * rank)
    wide = dot(left, (iota(spot, 1) // rank == iota(spot, 0)).astype(F32), HIGHEST)
    tall = jnp.broadcast_to(wide[:, None, :], (count, rank, rank * rank))
    tall = tall.reshape(count * rank, rank * rank)
    spot = (count * rank, rank * rank)
    tall = jnp.where(iota(spot, 0) % rank == iota(spot, 1) % rank, tall, 0.0)
    mixer = dot(tall, outer_proj[...].astype(F32), HIGHEST).reshape(count, rank, channels)
    high, low = (part.astype(F32) for part in split(mixer))
    mixer = jnp.concatenate([high, high, low, jnp.zeros_like(low)], axis=1).astype(BF16)
    high, low = (part.astype(F32) for part in split(right[...]))
    spread = jnp.concatenate([high, low, high, jnp.zeros_like(low)], axis=1).astype(BF16)
    head_of = iota((1, lanes), 1) // count
    row_of = iota((1, lanes), 1) - head_of * count
    expand = head_of == iota((heads, lanes), 0)
    high, low = split(dot_tn(bias_proj[...], expand.astype(F32), HIGHEST))
    weights = jnp.concatenate([high, high, low], axis=0)
    apart = jnp.sum(jnp.where(expand, column_of(chain_weight[...]), 0.0), axis=0, keepdims=True)
    chains = jnp.where(row_of == iota((count, lanes), 0), rows_column(query_chain[...]), 0)
    chains = jnp.sum(chains, axis=0, keepdims=True)
    bias = jnp.zeros((key_count, lanes), F32)
    copies = []
    for start in range(0, count, GROUP):
        indices = range(start, start + GROUP)
        updates = dot(spread, jnp.concatenate([mixer[index] for index in indices], axis=1))
        terms = []
        for index in indices:
            spot = (index // rows, index % rows)
            place = (index - start) * channels
            fresh = pair[spot] + updates[:, place : place + channels]
            fresh_scratch[index] = fresh
            copy = pltpu.make_async_copy(fresh_scratch.at[index], pair_out.at[spot], sems.at[index])
            copy.start()
            copies.append(copy)
            high, low = split(fresh)
            terms.append(jnp.concatenate([high, low, high], axis=1))
        here = dot(jnp.concatenate(terms, axis=0), weights)
        for index in indices:
            place = (index - start) * key_count
            bias = jnp.where(row_of == index, here[place : place + key_count], bias)
    bias = bias + jnp.where(column_of(key_chain[...]) != chains, apart, 0.0)
    high, low = split(bias)
    terms_out[...] = jnp.concatenate([high, low], axis=1)
    for copy in copies:
        copy.wait()


def listed(refs):
    values = []
    for ref in refs:
        values += [ref[...]] if len(ref.shape) == 2 else [ref[i] for i in range(ref.shape[0])]
    return values


def gathered(pieces, start, stop):
    if len(pieces) == 1:
        return pieces[0][:, start:stop]
    col = lax.axis_index("col")
    ours = listed(pieces[:3])
    share = ours[0].shape[1]
    values = [value for both in zip(ours, listed(pieces[3:])) for value in both]
    blocks = []
    for target in range(start // share, stop // share):
        chosen = values[0]
        for index in range(1, len(values)):
            chosen = jnp.where((col ^ target) == index, values[index], chosen)
        blocks.append(chosen)
    return jnp.concatenate(blocks, axis=1)


def attend_kernel(pieces, halves, biases, part_out, heads, count):
    row = lax.axis_index("row")
    _, model = halves[0].shape
    head = model // heads
    lanes = heads * count
    query = gathered(pieces, 0, model)
    biases = [bias[:, :lanes].astype(F32) + bias[:, lanes:].astype(F32) for bias in biases]
    firsts = [ref[...] for ref in halves[::2]]
    seconds = [ref[...] for ref in halves[1::2]]
    keys = [jnp.where(row == 0, first, second) for first, second in zip(firsts, seconds)]
    values = [jnp.where(row == 0, second, first) for first, second in zip(firsts, seconds)]
    head_of = iota((1, model), 1) // head
    spread = jnp.concatenate(
        [jnp.where(head_of == index, query, jnp.zeros_like(query)) for index in range(heads)],
        axis=0,
    )
    scale = 1.0 / math.sqrt(head)
    scores = [dot_nt(key, spread) * scale + bias for key, bias in zip(keys, biases)]
    peak = functools.reduce(jnp.maximum, [jnp.max(score, axis=0, keepdims=True) for score in scores])
    exponents = [jnp.exp(score - peak) for score in scores]
    total = sum(jnp.sum(exponent, axis=0, keepdims=True) for exponent in exponents)
    weights = jnp.concatenate([exponent.astype(BF16) for exponent in exponents], axis=0)
    summed = dot_tn(weights, jnp.concatenate(values, axis=0))
    taken = summed[:count]
    for index in range(1, heads):
        taken = jnp.where(head_of == index, summed[index * count : (index + 1) * count], taken)
    part_out[:, :model] = taken.astype(BF16)
    row_of = iota((1, lanes), 1) % count
    keep = row_of == iota((count, lanes), 0)
    source = iota((lanes, 1), 0) // count
    stats = jnp.zeros((count, LANES), F32)
    for index, term in enumerate(terms_of(peak, 3) + terms_of(total, 2)):
        target = (source + index * TERM == iota((lanes, LANES), 1)).astype(BF16)
        stats = stats + dot(jnp.where(keep, term, 0.0).astype(BF16), target)
    part_out[:, model:] = stats.astype(BF16)


def terms_of(value, count):
    terms = []
    for _ in range(count):
        term = value.astype(BF16).astype(F32)
        terms.append(term)
        value = value - term
    return terms


def merged(parts, heads):
    model = parts[0].shape[1] - LANES
    count = parts[0].shape[0]
    term = iota((LANES, 1), 0)
    place = iota((1, model), 1) // (model // heads)
    kind = term // TERM
    wanted = term - kind * TERM
    for_peak = (jnp.where(kind < 3, wanted, -1) == place).astype(BF16)
    for_total = (jnp.where((kind >= 3) & (kind < 5), wanted, -1) == place).astype(BF16)
    stats = jnp.concatenate([part[:, model:] for part in parts], axis=0)
    peaks, totals = dot(stats, for_peak), dot(stats, for_total)
    cut = lambda array, index: array[index * count : (index + 1) * count]
    peak = tree(jnp.maximum, [cut(peaks, index) for index in range(len(parts))])
    scales = [jnp.exp(cut(peaks, index) - peak) for index in range(len(parts))]
    total = tree(jnp.add, [scale * cut(totals, index) for index, scale in enumerate(scales)])
    summed = tree(jnp.add, [scale * part[:, :model].astype(F32) for scale, part in zip(scales, parts)])
    return summed / total


def tree(combine, values):
    while len(values) > 1:
        values = [
            combine(*values[index : index + 2]) if index + 1 < len(values) else values[index]
            for index in range(0, len(values), 2)
        ]
    return values[0]


def gate_kernel(*refs):
    pieces, gate_out = refs[:-1], refs[-1]
    model = gate_out.shape[1]
    gate_out[...] = jax.nn.sigmoid(gathered(pieces, model, 2 * model).astype(F32))


def finish_kernel(gate, parts, out_proj, update_out, heads):
    attended = (merged(listed(parts), heads) * gate[...]).astype(BF16)
    update_out[...] = dot(attended, out_proj[...]).astype(BF16)


def exchanged(value, axis, flip):
    size = lax.axis_size(axis)
    return lax.ppermute(value, axis, [(index, index ^ flip) for index in range(size)])


def on_device(
    pair_block,
    query_single,
    key_single,
    query_chain,
    key_chain,
    query_mask,
    key_mask,
    timestep,
    time_table,
    norm_gain,
    left_proj,
    right_proj,
    outer_proj,
    bias_proj,
    chain_weight,
    query_proj,
    kv_proj,
    out_proj,
):
    slabs, rows, model = query_single.shape
    count = slabs * rows
    key_count = key_single.shape[0]
    heads = chain_weight.shape[0]
    channels = pair_block.shape[-1]
    rank = left_proj.shape[1]
    lanes = heads * count
    cols = lax.axis_size("col")
    direct = cols == 8
    grant = pltpu.CompilerParams(vmem_limit_bytes=16 << 20)
    now = (query_mask, query_single, time_table, norm_gain, query_proj.T)
    later = (key_single, kv_proj, key_mask.reshape(1, key_count), right_proj.T)
    shape_of = lambda array: jax.ShapeDtypeStruct(array.shape, array.dtype)
    scratch_of = lambda array: pltpu.VMEM(array.shape, array.dtype)

    query_part, query_norm, time_row, gain, *later = pl.pallas_call(
        query_kernel,
        out_shape=(
            jax.ShapeDtypeStruct((count, query_proj.shape[1]), BF16),
            jax.ShapeDtypeStruct((count, model), BF16),
            jax.ShapeDtypeStruct((1, model), F32),
            shape_of(norm_gain),
        )
        + tuple(shape_of(array) for array in later),
        in_specs=[SMEM] + [HBM] * 9,
        out_specs=[VMEM] * 8,
        scratch_shapes=[
            scratch_of(query_mask),
            scratch_of(query_single),
            scratch_of(time_table),
            scratch_of(query_proj.T),
            pltpu.SemaphoreType.DMA((9,)),
        ],
        compiler_params=grant,
        name="query",
    )(timestep, *[pltpu.with_memory_space_constraint(array, pltpu.HBM) for array in now + later])

    if direct:
        beside = exchanged(query_part, "col", 2)

    half, right = pl.pallas_call(
        key_kernel,
        out_shape=(
            jax.ShapeDtypeStruct((key_count, kv_proj.shape[1]), BF16),
            jax.ShapeDtypeStruct((key_count, rank), F32),
        ),
        in_specs=[VMEM] * 6,
        out_specs=(VMEM, VMEM),
        compiler_params=grant,
        name="keys",
    )(time_row, gain, *later)
    halves = [half, exchanged(half, "row", 1)]
    if direct:
        far = exchanged(half, "col", 1)
        halves += [far, exchanged(far, "row", 1)]

    new_pair, bias = pl.pallas_call(
        pair_kernel,
        out_shape=(
            jax.ShapeDtypeStruct(pair_block.shape, F32),
            jax.ShapeDtypeStruct((key_count, 2 * lanes), BF16),
        ),
        in_specs=[VMEM] * 9,
        out_specs=(HBM, VMEM),
        scratch_shapes=[
            pltpu.VMEM((count, key_count, channels), F32),
            pltpu.SemaphoreType.DMA((count,)),
        ],
        compiler_params=grant,
        name="pairs",
    )(
        chain_weight.reshape(1, heads),
        query_chain,
        query_norm,
        left_proj.T,
        outer_proj,
        bias_proj.T,
        right,
        key_chain.reshape(1, key_count),
        pair_block,
    )
    if direct:
        biases = [bias, exchanged(bias, "col", 1)]
        across = exchanged(jnp.stack([query_part, beside]), "col", 4)
        ours = jnp.stack([query_part, beside, across[0], across[1]])
        pieces = [query_part, beside, across, exchanged(ours, "col", 1)]
    else:
        biases = [bias]
        pieces = [lax.all_gather(query_part, "col", axis=1, tiled=True)]

    def attend_body(*refs):
        n, k = len(pieces), len(pieces) + len(halves)
        attend_kernel(refs[:n], refs[n:k], refs[k:-1], refs[-1], heads, count)

    part = pl.pallas_call(
        attend_body,
        out_shape=jax.ShapeDtypeStruct((count, model + LANES), BF16),
        in_specs=[VMEM] * (len(pieces) + len(halves) + len(biases)),
        out_specs=VMEM,
        compiler_params=grant,
        name="attend",
    )(*pieces, *halves, *biases)

    if direct:
        parts = [part] + [exchanged(part, "col", flip) for flip in (2, 4, 6)]
    else:
        parts = [lax.all_gather(part, "col")]

    gate = pl.pallas_call(
        gate_kernel,
        out_shape=jax.ShapeDtypeStruct((count, model), F32),
        in_specs=[VMEM] * len(pieces),
        out_specs=VMEM,
        compiler_params=grant,
        name="gate",
    )(*pieces)

    def finish_body(gate, *refs):
        finish_kernel(gate, refs[:-2], *refs[-2:], heads)

    update = pl.pallas_call(
        finish_body,
        out_shape=jax.ShapeDtypeStruct((count, model), BF16),
        in_specs=[VMEM] * (len(parts) + 2),
        out_specs=VMEM,
        compiler_params=grant,
        name="finish",
    )(gate, *parts, out_proj)
    return (new_pair, update.reshape(slabs, rows, model))


def solution(mesh):
    return jax.shard_map(
        on_device,
        mesh=mesh,
        in_specs=(
            P("grp", "row", "col", None),
            P("grp", "row", None),
            P(("grp", "col"), None),
            P("grp", "row"),
            P(("grp", "col")),
            P("grp", "row"),
            P(("grp", "col")),
            P("grp"),
            P(),
            P(),
            P(),
            P(),
            P(),
            P(),
            P(),
            P(None, "col"),
            P(None, "row"),
            P(),
        ),
        out_specs=(P("grp", "row", "col", None), P("grp", "row", None)),
        check_vma=False,
    )
```

```python
import functools
import math

import jax
import jax.numpy as jnp
from jax import lax
from jax.experimental import pallas as pl
from jax.experimental.pallas import tpu as pltpu
from jax.sharding import PartitionSpec as P


EPSILON = 1e-05
LANES = 128
TERM = LANES // 5
GROUP = 4
VMEM = pl.BlockSpec(memory_space=pltpu.VMEM)
HBM = pl.BlockSpec(memory_space=pltpu.HBM)
SMEM = pl.BlockSpec(memory_space=pltpu.SMEM)
F32 = jnp.float32
BF16 = jnp.bfloat16


def dot(left, right, precision=None):
    return jnp.dot(left, right, preferred_element_type=F32, precision=precision)


def dot_nt(left, right):
    return lax.dot_general(left, right, (((1,), (1,)), ((), ())), preferred_element_type=F32)


def dot_tn(left, right, precision=None):
    return lax.dot_general(
        left, right, (((0,), (0,)), ((), ())), preferred_element_type=F32, precision=precision
    )


def iota(shape, axis):
    return lax.broadcasted_iota(jnp.int32, shape, axis)


def split(value):
    high = value.astype(BF16)
    return high, (value - high.astype(F32)).astype(BF16)


def normalized(features, gain):
    average = jnp.mean(features, axis=-1, keepdims=True)
    centred = features - average
    spread = jnp.mean(centred * centred, axis=-1, keepdims=True)
    return (centred * lax.rsqrt(spread + EPSILON) * gain).astype(BF16)


def column_of(row):
    count = row.shape[1]
    square = (count, count)
    return jnp.sum(jnp.where(iota(square, 0) == iota(square, 1), row, 0), axis=1, keepdims=True)


def rows_column(table):
    return jnp.concatenate([column_of(table[i : i + 1]) for i in range(table.shape[0])], axis=0)


def query_kernel(*refs):
    step, mask, single, table, gain, proj = refs[:6]
    later = refs[6:10]
    part_out, norm_out, time_out, gain_out = refs[10:14]
    later_out = refs[14:18]
    mask_in, single_in, table_in, proj_in, sems = refs[18:]
    sources = (mask, single, table, gain, proj) + later
    targets = (mask_in, single_in, table_in, gain_out, proj_in) + later_out
    copies = [
        pltpu.make_async_copy(source, target, sems.at[index])
        for index, (source, target) in enumerate(zip(sources, targets))
    ]
    for copy in copies:
        copy.start()
    for copy in copies[:4]:
        copy.wait()
    slabs, rows, width = single.shape
    features = single_in[...].astype(F32).reshape(slabs * rows, width)
    kept = rows_column(mask_in[...].astype(F32))
    held = table_in[...].astype(F32)
    time_row = jnp.sum(jnp.where(iota(held.shape, 0) == step[0], held, 0.0), axis=0, keepdims=True)
    time_out[...] = time_row
    norm = normalized(features + kept * time_row, gain_out[...].reshape(1, width))
    norm_out[...] = norm
    copies[4].wait()
    part_out[...] = dot_nt(norm, proj_in[...]).astype(BF16)
    for copy in copies[5:]:
        copy.wait()


def key_kernel(time_row, gain, single, proj, mask, right_proj, half_out, right_out):
    kept = column_of(mask[...].astype(F32))
    features = single[...].astype(F32) + kept * time_row[...]
    norm = normalized(features, gain[...].reshape(1, features.shape[1]))
    half_out[...] = dot(norm, proj[...]).astype(BF16)
    right_out[...] = dot_nt(norm, right_proj[...])


def pair_kernel(
    chain_weight,
    query_chain,
    query_norm,
    left_proj,
    outer_proj,
    bias_proj,
    right,
    key_chain,
    pair,
    pair_out,
    terms_out,
    bias_scratch,
):
    slabs, rows = query_chain.shape
    count = slabs * rows
    rank = left_proj.shape[0]
    heads, channels = bias_proj.shape
    key_count = right.shape[0]
    lanes = heads * count
    left = dot_nt(query_norm[...], left_proj[...])
    spot = (rank, rank * rank)
    repeat = (iota(spot, 1) // rank == iota(spot, 0)).astype(BF16)
    spot = (count * rank, rank * rank)
    diagonal = iota(spot, 0) % rank == iota(spot, 1) % rank
    tall = []
    for term in split(left):
        wide = jnp.broadcast_to(dot(term, repeat)[:, None, :], (count, rank, rank * rank))
        tall.append(jnp.where(diagonal, wide.reshape(spot), 0.0).astype(BF16))
    outer = outer_proj[...]
    mixer = dot(jnp.concatenate(tall, axis=1), jnp.concatenate([outer, outer], axis=0))
    high, low = (part.astype(F32) for part in split(mixer.reshape(count, rank, channels)))
    mixer = jnp.concatenate([high, high, low, jnp.zeros_like(low)], axis=1).astype(BF16)
    high, low = (part.astype(F32) for part in split(right[...]))
    spread = jnp.concatenate([high, low, high, jnp.zeros_like(low)], axis=1).astype(BF16)
    head_of = iota((1, lanes), 1) // count
    row_of = iota((1, lanes), 1) - head_of * count
    expand = head_of == iota((heads, lanes), 0)
    high, low = (dot_tn(term, expand.astype(BF16)).astype(BF16) for term in split(bias_proj[...]))
    weights = jnp.concatenate([high, high, low], axis=0)
    apart = jnp.sum(jnp.where(expand, column_of(chain_weight[...]), 0.0), axis=0, keepdims=True)
    chains = jnp.where(row_of == iota((count, lanes), 0), rows_column(query_chain[...]), 0)
    chains = jnp.sum(chains, axis=0, keepdims=True)
    for start in range(0, count, GROUP):
        indices = range(start, start + GROUP)
        updates = dot(spread, jnp.concatenate([mixer[index] for index in indices], axis=1))
        terms = []
        for index in indices:
            spot = (index // rows, index % rows)
            place = (index - start) * channels
            fresh = pair[spot] + updates[:, place : place + channels]
            pair_out[spot] = fresh
            high, low = split(fresh)
            terms.append(jnp.concatenate([high, low, high], axis=1))
        here = dot(jnp.concatenate(terms, axis=0), weights)
        for index in indices:
            place = (index - start) * key_count
            wanted = jnp.broadcast_to(row_of == index, (key_count, lanes))
            pltpu.store(bias_scratch, here[place : place + key_count], mask=wanted)
    bias = bias_scratch[...] + jnp.where(column_of(key_chain[...]) != chains, apart, 0.0)
    terms_out[...] = jnp.concatenate(split(bias), axis=1)


def listed(refs):
    values = []
    for ref in refs:
        values += [ref[...]] if len(ref.shape) == 2 else [ref[i] for i in range(ref.shape[0])]
    return values


def gathered(pieces, flips, start, stop):
    values = listed(pieces)
    if len(values) == 1:
        return values[0][:, start:stop]
    col = lax.axis_index("col")
    share = values[0].shape[1]
    blocks = []
    for target in range(start // share, stop // share):
        chosen = values[0]
        for flip, value in zip(flips[1:], values[1:]):
            chosen = jnp.where((col ^ target) == flip, value, chosen)
        blocks.append(chosen)
    return jnp.concatenate(blocks, axis=1)


def attend_kernel(pieces, flips, halves, biases, part_out, heads, count):
    row = lax.axis_index("row")
    query = gathered(pieces, flips, 0, halves[0].shape[1])

    @pl.when(row == 0)
    def _():
        attend(query, halves[::2], halves[1::2], biases, part_out, heads, count)

    @pl.when(row != 0)
    def _():
        attend(query, halves[1::2], halves[::2], biases, part_out, heads, count)


def attend(query, keys, values, biases, part_out, heads, count):
    model = query.shape[1]
    head = model // heads
    lanes = heads * count
    biases = [bias[:, :lanes].astype(F32) + bias[:, lanes:].astype(F32) for bias in biases]
    head_of = iota((1, model), 1) // head
    spread = jnp.concatenate(
        [jnp.where(head_of == index, query, jnp.zeros_like(query)) for index in range(heads)],
        axis=0,
    )
    scale = 1.0 / math.sqrt(head)
    scores = [dot_nt(key[...], spread) * scale + bias for key, bias in zip(keys, biases)]
    peak = functools.reduce(jnp.maximum, [jnp.max(score, axis=0, keepdims=True) for score in scores])
    exponents = [jnp.exp(score - peak) for score in scores]
    total = sum(jnp.sum(exponent, axis=0, keepdims=True) for exponent in exponents)
    weights = jnp.concatenate(exponents, axis=0).T.astype(BF16)
    value = jnp.concatenate([value[...] for value in values], axis=0)
    group = LANES // head
    within = iota((1, LANES), 1) // head
    for first in range(0, heads, group):
        place = slice(first * head, first * head + LANES)
        summed = dot(weights[first * count : (first + group) * count], value[:, place])
        taken = summed[:count]
        for index in range(1, group):
            taken = jnp.where(within == index, summed[index * count : (index + 1) * count], taken)
        part_out[:, place] = taken.astype(BF16)
    row_of = iota((1, lanes), 1) % count
    keep = row_of == iota((count, lanes), 0)
    source = iota((lanes, 1), 0) // count
    stats = jnp.zeros((count, LANES), F32)
    for index, term in enumerate(terms_of(peak, 3) + terms_of(total, 2)):
        target = (source + index * TERM == iota((lanes, LANES), 1)).astype(BF16)
        stats = stats + dot(jnp.where(keep, term, 0.0).astype(BF16), target)
    part_out[:, model:] = stats.astype(BF16)


def terms_of(value, count):
    terms = []
    for _ in range(count):
        term = value.astype(BF16).astype(F32)
        terms.append(term)
        value = value - term
    return terms


def spreaders(model, heads):
    term = iota((LANES, 1), 0)
    place = iota((1, model), 1) // (model // heads)
    kind = term // TERM
    wanted = term - kind * TERM
    for_peak = jnp.where(kind < 3, wanted, -1) == place
    for_total = jnp.where((kind >= 3) & (kind < 5), wanted, -1) == place
    return for_peak.astype(BF16), for_total.astype(BF16)


def merged(parts, spreads):
    model = parts[0].shape[1] - LANES
    count = parts[0].shape[0]
    stats = jnp.concatenate([part[:, model:] for part in parts], axis=0)
    peaks, totals = dot(stats, spreads[0]), dot(stats, spreads[1])
    cut = lambda array, index: array[index * count : (index + 1) * count]
    peak = tree(jnp.maximum, [cut(peaks, index) for index in range(len(parts))])
    scales = [jnp.exp(cut(peaks, index) - peak) for index in range(len(parts))]
    total = tree(jnp.add, [scale * cut(totals, index) for index, scale in enumerate(scales)])
    summed = tree(jnp.add, [scale * part[:, :model].astype(F32) for scale, part in zip(scales, parts)])
    return summed / total


def tree(combine, values):
    while len(values) > 1:
        values = [
            combine(*values[index : index + 2]) if index + 1 < len(values) else values[index]
            for index in range(0, len(values), 2)
        ]
    return values[0]


def gate_kernel(fresh, *refs, flips, heads):
    pieces, gate_out, spread_out, pair_out, sem = refs[:-4], *refs[-4:]
    copy = pltpu.make_async_copy(fresh, pair_out, sem)
    copy.start()
    model = gate_out.shape[1]
    spread_out[0], spread_out[1] = spreaders(model, heads)
    gate_out[...] = jax.nn.sigmoid(gathered(pieces, flips, model, 2 * model).astype(F32))
    copy.wait()


def finish_kernel(gate, spreads, *refs):
    parts, out_proj, update_out = refs[:-2], *refs[-2:]
    attended = (merged(listed(parts), spreads) * gate[...]).astype(BF16)
    update_out[...] = dot(attended, out_proj[...]).astype(BF16)


def exchanged(value, axis, flip):
    size = lax.axis_size(axis)
    return lax.ppermute(value, axis, [(index, index ^ flip) for index in range(size)])


def spread_over(part):
    held, pieces, flips = [part], [part], [0]
    for group in PLAN:
        count = len(held)
        sent = held[0] if count == 1 else jnp.stack(held)
        for flip in group:
            piece = exchanged(sent, "col", flip)
            pieces.append(piece)
            flips = flips + [flip ^ other for other in flips[:count]]
            held = held + ([piece] if count == 1 else [piece[i] for i in range(count)])
    return pieces, flips


def on_device(
    pair_block,
    query_single,
    key_single,
    query_chain,
    key_chain,
    query_mask,
    key_mask,
    timestep,
    time_table,
    norm_gain,
    left_proj,
    right_proj,
    outer_proj,
    bias_proj,
    chain_weight,
    query_proj,
    kv_proj,
    out_proj,
):
    slabs, rows, model = query_single.shape
    count = slabs * rows
    key_count = key_single.shape[0]
    heads = chain_weight.shape[0]
    rank = left_proj.shape[1]
    lanes = heads * count
    cols = lax.axis_size("col")
    direct = cols == 8
    grant = pltpu.CompilerParams(vmem_limit_bytes=16 << 20)
    now = (query_mask, query_single, time_table, norm_gain, query_proj.T)
    later = (key_single, kv_proj, key_mask.reshape(1, key_count), right_proj.T)
    shape_of = lambda array: jax.ShapeDtypeStruct(array.shape, array.dtype)
    scratch_of = lambda array: pltpu.VMEM(array.shape, array.dtype)

    query_part, query_norm, time_row, gain, *later = pl.pallas_call(
        query_kernel,
        out_shape=(
            jax.ShapeDtypeStruct((count, query_proj.shape[1]), BF16),
            jax.ShapeDtypeStruct((count, model), BF16),
            jax.ShapeDtypeStruct((1, model), F32),
            shape_of(norm_gain),
        )
        + tuple(shape_of(array) for array in later),
        in_specs=[SMEM] + [HBM] * 9,
        out_specs=[VMEM] * 8,
        scratch_shapes=[
            scratch_of(query_mask),
            scratch_of(query_single),
            scratch_of(time_table),
            scratch_of(query_proj.T),
            pltpu.SemaphoreType.DMA((9,)),
        ],
        compiler_params=grant,
        name="query",
    )(timestep, *[pltpu.with_memory_space_constraint(array, pltpu.HBM) for array in now + later])

    flips = [0]
    if direct:
        pieces, flips = spread_over(query_part)
    else:
        pieces = [lax.all_gather(query_part, "col", axis=1, tiled=True)]

    half, right = pl.pallas_call(
        key_kernel,
        out_shape=(
            jax.ShapeDtypeStruct((key_count, kv_proj.shape[1]), BF16),
            jax.ShapeDtypeStruct((key_count, rank), F32),
        ),
        in_specs=[VMEM] * 6,
        out_specs=(VMEM, VMEM),
        compiler_params=grant,
        name="keys",
    )(time_row, gain, *later)
    halves = [half, exchanged(half, "row", 1)]
    if direct:
        far = exchanged(half, "col", 1)
        halves += [far, exchanged(far, "row", 1)]

    fresh_pair, bias = pl.pallas_call(
        pair_kernel,
        out_shape=(
            jax.ShapeDtypeStruct(pair_block.shape, F32),
            jax.ShapeDtypeStruct((key_count, 2 * lanes), BF16),
        ),
        in_specs=[VMEM] * 9,
        out_specs=(VMEM, VMEM),
        scratch_shapes=[pltpu.VMEM((key_count, lanes), F32)],
        compiler_params=grant,
        name="pairs",
    )(
        chain_weight.reshape(1, heads),
        query_chain,
        query_norm,
        left_proj.T,
        outer_proj,
        bias_proj.T,
        right,
        key_chain.reshape(1, key_count),
        pair_block,
    )
    biases = [bias]
    if direct:
        biases.append(exchanged(bias, "col", 1))

    def attend_body(*refs):
        n, k = len(pieces), len(pieces) + len(halves)
        attend_kernel(refs[:n], flips, refs[n:k], refs[k:-1], refs[-1], heads, count)

    part = pl.pallas_call(
        attend_body,
        out_shape=jax.ShapeDtypeStruct((count, model + LANES), BF16),
        in_specs=[VMEM] * (len(pieces) + len(halves) + len(biases)),
        out_specs=VMEM,
        compiler_params=grant,
        name="attend",
    )(*pieces, *halves, *biases)

    if direct:
        parts = [part] + [exchanged(part, "col", flip) for flip in (2, 4, 6)]
    else:
        parts = [lax.all_gather(part, "col")]

    gate, spreads, new_pair = pl.pallas_call(
        functools.partial(gate_kernel, flips=flips, heads=heads),
        out_shape=(
            jax.ShapeDtypeStruct((count, model), F32),
            jax.ShapeDtypeStruct((2, LANES, model), BF16),
            jax.ShapeDtypeStruct(pair_block.shape, F32),
        ),
        in_specs=[VMEM] * (1 + len(pieces)),
        out_specs=(VMEM, VMEM, HBM),
        scratch_shapes=[pltpu.SemaphoreType.DMA],
        compiler_params=grant,
        name="gate",
    )(fresh_pair, *pieces)

    update = pl.pallas_call(
        finish_kernel,
        out_shape=jax.ShapeDtypeStruct((count, model), BF16),
        in_specs=[VMEM] * (len(parts) + 3),
        out_specs=VMEM,
        compiler_params=grant,
        name="finish",
    )(gate, spreads, *parts, out_proj)
    return (new_pair, update.reshape(slabs, rows, model))


PLAN = ((1,), (6, 4, 2))


def solution(mesh):
    return jax.shard_map(
        on_device,
        mesh=mesh,
        in_specs=(
            P("grp", "row", "col", None),
            P("grp", "row", None),
            P(("grp", "col"), None),
            P("grp", "row"),
            P(("grp", "col")),
            P("grp", "row"),
            P(("grp", "col")),
            P("grp"),
            P(),
            P(),
            P(),
            P(),
            P(),
            P(),
            P(),
            P(None, "col"),
            P(None, "row"),
            P(),
        ),
        out_specs=(P("grp", "row", "col", None), P("grp", "row", None)),
        check_vma=False,
    )
```

```python
import functools
import math

import jax
import jax.numpy as jnp
from jax import lax
from jax.experimental import pallas as pl
from jax.experimental.pallas import tpu as pltpu
from jax.sharding import PartitionSpec as P


EPSILON = 1e-05
LANES = 128
TERM = LANES // 5
GROUP = 4
STACK = 2
VMEM = pl.BlockSpec(memory_space=pltpu.VMEM)
HBM = pl.BlockSpec(memory_space=pltpu.HBM)
SMEM = pl.BlockSpec(memory_space=pltpu.SMEM)
F32 = jnp.float32
BF16 = jnp.bfloat16


def dot(left, right, precision=None):
    return jnp.dot(left, right, preferred_element_type=F32, precision=precision)


def dot_nt(left, right):
    return lax.dot_general(left, right, (((1,), (1,)), ((), ())), preferred_element_type=F32)


def dot_tn(left, right, precision=None):
    return lax.dot_general(
        left, right, (((0,), (0,)), ((), ())), preferred_element_type=F32, precision=precision
    )


def iota(shape, axis):
    return lax.broadcasted_iota(jnp.int32, shape, axis)


def split(value):
    high = value.astype(BF16)
    return high, (value - high.astype(F32)).astype(BF16)


def normalized(features, gain):
    average = jnp.mean(features, axis=-1, keepdims=True)
    centred = features - average
    spread = jnp.mean(centred * centred, axis=-1, keepdims=True)
    return (centred * lax.rsqrt(spread + EPSILON) * gain).astype(BF16)


def column_of(row):
    count = row.shape[1]
    square = (count, count)
    return jnp.sum(jnp.where(iota(square, 0) == iota(square, 1), row, 0), axis=1, keepdims=True)


def rows_column(table):
    return jnp.concatenate([column_of(table[i : i + 1]) for i in range(table.shape[0])], axis=0)


def query_kernel(*refs):
    step, mask, single, table, gain, proj = refs[:6]
    later = refs[6:10]
    part_out, norm_out, time_out, gain_out = refs[10:14]
    later_out = refs[14:18]
    mask_in, single_in, table_in, proj_in, sems = refs[18:]
    sources = (mask, single, table, gain, proj) + later
    targets = (mask_in, single_in, table_in, gain_out, proj_in) + later_out
    copies = [
        pltpu.make_async_copy(source, target, sems.at[index])
        for index, (source, target) in enumerate(zip(sources, targets))
    ]
    for copy in copies:
        copy.start()
    for copy in copies[:4]:
        copy.wait()
    slabs, rows, width = single.shape
    features = single_in[...].astype(F32).reshape(slabs * rows, width)
    kept = rows_column(mask_in[...].astype(F32))
    held = table_in[...].astype(F32)
    time_row = jnp.sum(jnp.where(iota(held.shape, 0) == step[0], held, 0.0), axis=0, keepdims=True)
    time_out[...] = time_row
    norm = normalized(features + kept * time_row, gain_out[...].reshape(1, width))
    norm_out[...] = norm
    copies[4].wait()
    part_out[...] = dot_nt(norm, proj_in[...]).astype(BF16)
    for copy in copies[5:]:
        copy.wait()


def key_kernel(time_row, gain, single, proj, mask, right_proj, half_out, right_out):
    kept = column_of(mask[...].astype(F32))
    features = single[...].astype(F32) + kept * time_row[...]
    norm = normalized(features, gain[...].reshape(1, features.shape[1]))
    half_out[...] = dot(norm, proj[...]).astype(BF16)
    right_out[...] = dot_nt(norm, right_proj[...])


def bias_kernel(
    chain_weight,
    query_chain,
    query_norm,
    left_proj,
    outer_proj,
    bias_proj,
    right,
    key_chain,
    pair,
    mixer_out,
    spread_out,
    terms_out,
    bias_scratch,
):
    slabs, rows = query_chain.shape
    count = slabs * rows
    rank = left_proj.shape[0]
    heads, channels = bias_proj.shape
    key_count = right.shape[0]
    lanes = heads * count
    left = dot_nt(query_norm[...], left_proj[...])
    spot = (rank, rank * rank)
    repeat = (iota(spot, 1) // rank == iota(spot, 0)).astype(BF16)
    spot = (count * rank, rank * rank)
    diagonal = iota(spot, 0) % rank == iota(spot, 1) % rank
    tall = []
    for term in split(left):
        wide = jnp.broadcast_to(dot(term, repeat)[:, None, :], (count, rank, rank * rank))
        tall.append(jnp.where(diagonal, wide.reshape(spot), 0.0).astype(BF16))
    outer = outer_proj[...]
    mixer = dot(jnp.concatenate(tall, axis=1), jnp.concatenate([outer, outer], axis=0))
    head_of = iota((1, lanes), 1) // count
    row_of = iota((1, lanes), 1) - head_of * count
    expand = head_of == iota((heads, lanes), 0)
    high, low = (dot_tn(term, expand.astype(BF16)).astype(BF16) for term in split(bias_proj[...]))
    weights = jnp.concatenate([high, high, low], axis=0)
    masked = lambda term: [jnp.where(row_of % GROUP == r, term, 0.0).astype(BF16) for r in range(GROUP)]
    wide = masked(high.astype(F32))
    wide = jnp.concatenate(wide + wide + masked(low.astype(F32)), axis=0)
    for start in range(0, count, GROUP * STACK):
        terms = []
        for first in range(start, start + GROUP * STACK, GROUP):
            both = [split(pair[index // rows, index % rows]) for index in range(first, first + GROUP)]
            highs, lows = [high for high, _ in both], [low for _, low in both]
            terms.append(jnp.concatenate(highs + lows + highs, axis=1))
        here = dot(jnp.concatenate(terms, axis=0), wide)
        for step in range(STACK):
            wanted = jnp.broadcast_to(row_of // GROUP == start // GROUP + step, (key_count, lanes))
            place = step * key_count
            pltpu.store(bias_scratch, here[place : place + key_count], mask=wanted)
    high, low = split(mixer)
    folded = dot(jnp.concatenate([high, low, high], axis=1), weights).reshape(count, rank, lanes)
    folded = sum(jnp.where(row_of == index, folded[index], 0.0) for index in range(count))
    stacked = lambda first, second, third, axis: jnp.concatenate(
        [term.astype(F32) for term in (first, second, third)] + [jnp.zeros(first.shape, F32)], axis=axis
    ).astype(BF16)
    high, low = split(right[...])
    spread = stacked(high, low, high, 1)
    spread_out[...] = spread
    high, low = split(mixer.reshape(count, rank, channels))
    mixer_out[...] = stacked(high, high, low, 1)
    high, low = split(folded)
    bias = bias_scratch[...] + dot(spread, stacked(high, high, low, 0))
    apart = jnp.sum(jnp.where(expand, column_of(chain_weight[...]), 0.0), axis=0, keepdims=True)
    chains = jnp.where(row_of == iota((count, lanes), 0), rows_column(query_chain[...]), 0)
    chains = jnp.sum(chains, axis=0, keepdims=True)
    bias = bias + jnp.where(column_of(key_chain[...]) != chains, apart, 0.0)
    terms_out[...] = jnp.concatenate(split(bias), axis=1)


def listed(refs):
    values = []
    for ref in refs:
        values += [ref[...]] if len(ref.shape) == 2 else [ref[i] for i in range(ref.shape[0])]
    return values


def gathered(pieces, flips, start, stop):
    values = listed(pieces)
    if len(values) == 1:
        return values[0][:, start:stop]
    col = lax.axis_index("col")
    share = values[0].shape[1]
    blocks = []
    for target in range(start // share, stop // share):
        chosen = values[0]
        for flip, value in zip(flips[1:], values[1:]):
            chosen = jnp.where((col ^ target) == flip, value, chosen)
        blocks.append(chosen)
    return jnp.concatenate(blocks, axis=1)


def attend_kernel(pieces, flips, halves, biases, part_out, heads, count):
    row = lax.axis_index("row")
    query = gathered(pieces, flips, 0, halves[0].shape[1])

    @pl.when(row == 0)
    def _():
        attend(query, halves[::2], halves[1::2], biases, part_out, heads, count)

    @pl.when(row != 0)
    def _():
        attend(query, halves[1::2], halves[::2], biases, part_out, heads, count)


def attend(query, keys, values, biases, part_out, heads, count):
    model = query.shape[1]
    head = model // heads
    lanes = heads * count
    biases = [bias[:, :lanes].astype(F32) + bias[:, lanes:].astype(F32) for bias in biases]
    head_of = iota((1, model), 1) // head
    spread = jnp.concatenate(
        [jnp.where(head_of == index, query, jnp.zeros_like(query)) for index in range(heads)],
        axis=0,
    )
    scale = 1.0 / math.sqrt(head)
    scores = [dot_nt(key[...], spread) * scale + bias for key, bias in zip(keys, biases)]
    peak = functools.reduce(jnp.maximum, [jnp.max(score, axis=0, keepdims=True) for score in scores])
    exponents = [jnp.exp(score - peak) for score in scores]
    total = sum(jnp.sum(exponent, axis=0, keepdims=True) for exponent in exponents)
    weights = jnp.concatenate(exponents, axis=0).T.astype(BF16)
    value = jnp.concatenate([value[...] for value in values], axis=0)
    group = LANES // head
    within = iota((1, LANES), 1) // head
    for first in range(0, heads, group):
        place = slice(first * head, first * head + LANES)
        summed = dot(weights[first * count : (first + group) * count], value[:, place])
        taken = summed[:count]
        for index in range(1, group):
            taken = jnp.where(within == index, summed[index * count : (index + 1) * count], taken)
        part_out[:, place] = taken.astype(BF16)
    row_of = iota((1, lanes), 1) % count
    keep = row_of == iota((count, lanes), 0)
    source = iota((lanes, 1), 0) // count
    stats = jnp.zeros((count, LANES), F32)
    for index, term in enumerate(terms_of(peak, 3) + terms_of(total, 2)):
        target = (source + index * TERM == iota((lanes, LANES), 1)).astype(BF16)
        stats = stats + dot(jnp.where(keep, term, 0.0).astype(BF16), target)
    part_out[:, model:] = stats.astype(BF16)


def terms_of(value, count):
    terms = []
    for _ in range(count):
        term = value.astype(BF16).astype(F32)
        terms.append(term)
        value = value - term
    return terms


def spreaders(model, heads):
    term = iota((LANES, 1), 0)
    place = iota((1, model), 1) // (model // heads)
    kind = term // TERM
    wanted = term - kind * TERM
    for_peak = jnp.where(kind < 3, wanted, -1) == place
    for_total = jnp.where((kind >= 3) & (kind < 5), wanted, -1) == place
    return for_peak.astype(BF16), for_total.astype(BF16)


def merged(parts, spreads):
    model = parts[0].shape[1] - LANES
    count = parts[0].shape[0]
    stats = jnp.concatenate([part[:, model:] for part in parts], axis=0)
    peaks, totals = dot(stats, spreads[0]), dot(stats, spreads[1])
    cut = lambda array, index: array[index * count : (index + 1) * count]
    peak = tree(jnp.maximum, [cut(peaks, index) for index in range(len(parts))])
    scales = [jnp.exp(cut(peaks, index) - peak) for index in range(len(parts))]
    total = tree(jnp.add, [scale * cut(totals, index) for index, scale in enumerate(scales)])
    summed = tree(jnp.add, [scale * part[:, :model].astype(F32) for scale, part in zip(scales, parts)])
    return summed / total


def tree(combine, values):
    while len(values) > 1:
        values = [
            combine(*values[index : index + 2]) if index + 1 < len(values) else values[index]
            for index in range(0, len(values), 2)
        ]
    return values[0]


def gate_kernel(pair, mixer, spread, *refs, flips, heads):
    pieces, gate_out, spread_out, pair_out, fresh, sems = refs[:-5], *refs[-5:]
    slabs, rows, _, channels = pair.shape
    keys = spread[...]
    copies = []
    for start in range(0, slabs * rows, 2):
        both = dot(keys, jnp.concatenate([mixer[start], mixer[start + 1]], axis=1))
        for index in (start, start + 1):
            spot = (index // rows, index % rows)
            place = (index - start) * channels
            fresh[spot] = pair[spot] + both[:, place : place + channels]
        if (start + 2) % rows == 0:
            slab = start // rows
            copies.append(pltpu.make_async_copy(fresh.at[slab], pair_out.at[slab], sems.at[slab]))
            copies[-1].start()
    model = gate_out.shape[1]
    spread_out[0], spread_out[1] = spreaders(model, heads)
    gate_out[...] = jax.nn.sigmoid(gathered(pieces, flips, model, 2 * model).astype(F32))
    for copy in copies:
        copy.wait()


def finish_kernel(gate, spreads, *refs):
    parts, out_proj, update_out = refs[:-2], *refs[-2:]
    attended = (merged(listed(parts), spreads) * gate[...]).astype(BF16)
    update_out[...] = dot(attended, out_proj[...]).astype(BF16)


def exchanged(value, axis, flip):
    size = lax.axis_size(axis)
    return lax.ppermute(value, axis, [(index, index ^ flip) for index in range(size)])


def spread_over(part):
    held, pieces, flips = [part], [part], [0]
    for group in PLAN:
        count = len(held)
        sent = held[0] if count == 1 else jnp.stack(held)
        for flip in group:
            piece = exchanged(sent, "col", flip)
            pieces.append(piece)
            flips = flips + [flip ^ other for other in flips[:count]]
            held = held + ([piece] if count == 1 else [piece[i] for i in range(count)])
    return pieces, flips


def on_device(
    pair_block,
    query_single,
    key_single,
    query_chain,
    key_chain,
    query_mask,
    key_mask,
    timestep,
    time_table,
    norm_gain,
    left_proj,
    right_proj,
    outer_proj,
    bias_proj,
    chain_weight,
    query_proj,
    kv_proj,
    out_proj,
):
    slabs, rows, model = query_single.shape
    count = slabs * rows
    key_count = key_single.shape[0]
    heads = chain_weight.shape[0]
    channels = pair_block.shape[-1]
    rank = left_proj.shape[1]
    lanes = heads * count
    cols = lax.axis_size("col")
    direct = cols == 8
    grant = pltpu.CompilerParams(vmem_limit_bytes=16 << 20)
    now = (query_mask, query_single, time_table, norm_gain, query_proj.T)
    later = (key_single, kv_proj, key_mask.reshape(1, key_count), right_proj.T)
    shape_of = lambda array: jax.ShapeDtypeStruct(array.shape, array.dtype)
    scratch_of = lambda array: pltpu.VMEM(array.shape, array.dtype)

    query_part, query_norm, time_row, gain, *later = pl.pallas_call(
        query_kernel,
        out_shape=(
            jax.ShapeDtypeStruct((count, query_proj.shape[1]), BF16),
            jax.ShapeDtypeStruct((count, model), BF16),
            jax.ShapeDtypeStruct((1, model), F32),
            shape_of(norm_gain),
        )
        + tuple(shape_of(array) for array in later),
        in_specs=[SMEM] + [HBM] * 9,
        out_specs=[VMEM] * 8,
        scratch_shapes=[
            scratch_of(query_mask),
            scratch_of(query_single),
            scratch_of(time_table),
            scratch_of(query_proj.T),
            pltpu.SemaphoreType.DMA((9,)),
        ],
        compiler_params=grant,
        name="query",
    )(timestep, *[pltpu.with_memory_space_constraint(array, pltpu.HBM) for array in now + later])

    flips = [0]
    if direct:
        pieces, flips = spread_over(query_part)
    else:
        pieces = [lax.all_gather(query_part, "col", axis=1, tiled=True)]

    half, right = pl.pallas_call(
        key_kernel,
        out_shape=(
            jax.ShapeDtypeStruct((key_count, kv_proj.shape[1]), BF16),
            jax.ShapeDtypeStruct((key_count, rank), F32),
        ),
        in_specs=[VMEM] * 6,
        out_specs=(VMEM, VMEM),
        compiler_params=grant,
        name="keys",
    )(time_row, gain, *later)
    halves = [half, exchanged(half, "row", 1)]
    if direct:
        far = exchanged(half, "col", 1)
        halves += [far, exchanged(far, "row", 1)]

    mixer, spread, bias = pl.pallas_call(
        bias_kernel,
        out_shape=(
            jax.ShapeDtypeStruct((count, 4 * rank, channels), BF16),
            jax.ShapeDtypeStruct((key_count, 4 * rank), BF16),
            jax.ShapeDtypeStruct((key_count, 2 * lanes), BF16),
        ),
        in_specs=[VMEM] * 9,
        out_specs=(VMEM, VMEM, VMEM),
        scratch_shapes=[pltpu.VMEM((key_count, lanes), F32)],
        compiler_params=grant,
        name="biases",
    )(
        chain_weight.reshape(1, heads),
        query_chain,
        query_norm,
        left_proj.T,
        outer_proj,
        bias_proj.T,
        right,
        key_chain.reshape(1, key_count),
        pair_block,
    )
    biases = [bias]
    if direct:
        biases.append(exchanged(bias, "col", 1))

    def attend_body(*refs):
        n, k = len(pieces), len(pieces) + len(halves)
        attend_kernel(refs[:n], flips, refs[n:k], refs[k:-1], refs[-1], heads, count)

    part = pl.pallas_call(
        attend_body,
        out_shape=jax.ShapeDtypeStruct((count, model + LANES), BF16),
        in_specs=[VMEM] * (len(pieces) + len(halves) + len(biases)),
        out_specs=VMEM,
        compiler_params=grant,
        name="attend",
    )(*pieces, *halves, *biases)

    if direct:
        parts = [part] + [exchanged(part, "col", flip) for flip in (2, 4, 6)]
    else:
        parts = [lax.all_gather(part, "col")]

    gate, spreads, new_pair = pl.pallas_call(
        functools.partial(gate_kernel, flips=flips, heads=heads),
        out_shape=(
            jax.ShapeDtypeStruct((count, model), F32),
            jax.ShapeDtypeStruct((2, LANES, model), BF16),
            jax.ShapeDtypeStruct(pair_block.shape, F32),
        ),
        in_specs=[VMEM] * (3 + len(pieces)),
        out_specs=(VMEM, VMEM, HBM),
        scratch_shapes=[pltpu.VMEM(pair_block.shape, F32), pltpu.SemaphoreType.DMA((slabs,))],
        compiler_params=grant,
        name="gate",
    )(pair_block, mixer, spread, *pieces)

    update = pl.pallas_call(
        finish_kernel,
        out_shape=jax.ShapeDtypeStruct((count, model), BF16),
        in_specs=[VMEM] * (len(parts) + 3),
        out_specs=VMEM,
        compiler_params=grant,
        name="finish",
    )(gate, spreads, *parts, out_proj)
    return (new_pair, update.reshape(slabs, rows, model))


PLAN = ((1,), (6, 4, 2))


def solution(mesh):
    return jax.shard_map(
        on_device,
        mesh=mesh,
        in_specs=(
            P("grp", "row", "col", None),
            P("grp", "row", None),
            P(("grp", "col"), None),
            P("grp", "row"),
            P(("grp", "col")),
            P("grp", "row"),
            P(("grp", "col")),
            P("grp"),
            P(),
            P(),
            P(),
            P(),
            P(),
            P(),
            P(),
            P(None, "col"),
            P(None, "row"),
            P(),
        ),
        out_specs=(P("grp", "row", "col", None), P("grp", "row", None)),
        check_vma=False,
    )
```
